768 devices in a mesh: dp: 192 (over z, y, core), tensor: 4 (over x).
Axes of the slice: x: 4, y: 8, z: 12, core: 2. Of those that a mesh axis runs over, the one named last changes fastest.
Arguments:
- hidden: bfloat16 [24576, 8192], P('dp'), may hold values from -50 to 50
- gain: float32 [8192], replicated, may hold values from 0.5 to 1.5
- w_key: bfloat16 [8192, 512], P(None, 'tensor'), may hold values from -3 to 3
- grad_key: bfloat16 [24576, 512], P('dp', 'tensor'), may hold values from -0.119628906 to 0.119628906
- counts: int32 [192], P('dp'), may hold values from 32 to 128, as said below
Outputs:
- key_grad: float32 [8256, 512], P('dp', 'tensor')
- normed_grad: bfloat16 [24576, 8192], P('dp', 'tensor')
The draws below stay inside these ranges and needn't reach their ends.
Inputs may be any that keep to these rules, and one draw needn't show every extreme that they name: Tokens past counts of a bin are padding. At least one bin is full and one holds exactly 32 real tokens.
All inputs are finite; a program needn't handle non-finite values.
Results may differ from the reference program's by a relative error of at most 0.012.
Values may be sent and summed in bfloat16 or wider, within the bound.
A program may use at most 32 MiB of HBM per device.

```python
import math
import jax
import jax.numpy as jnp
from jax import lax

D = 8192
HD = 128
TOK_DEV = 128
KV = 4
BINS = 192
TOKENS = 24576
D_PAD = 8256


def draw_hidden(key, part):
    subkeys = jax.random.split(key, 3)
    row_scale = jnp.exp(jax.random.uniform(subkeys[0], (TOKENS, 1), jnp.float32, 0.0, math.log(10.0)))
    col_scale = jnp.exp(jax.random.uniform(subkeys[1], (1, D), jnp.float32, 0.0, math.log(10.0)))
    base_draw = jnp.clip(jax.random.normal(subkeys[2], (TOKENS, D), jnp.float32), -5.0, 5.0)
    return (0.1 * base_draw * row_scale * col_scale).astype(jnp.bfloat16)


def draw_counts(key, part):
    subkeys = jax.random.split(key, 4)
    bin_index = jnp.arange(BINS)
    rising = TOK_DEV // 4 + bin_index * (TOK_DEV // 2) // max(BINS - 1, 1)
    jitter = jax.random.randint(subkeys[0], (BINS,), 0, TOK_DEV // 8 + 1)
    values = jnp.minimum(rising + jitter, TOK_DEV)
    full_bins = jax.random.randint(subkeys[1], (BINS,), 0, 8) == 0
    top_bin = jax.random.randint(subkeys[2], (), 0, BINS)
    low_bin = (top_bin + 1 + jax.random.randint(subkeys[3], (), 0, max(BINS - 1, 1))) % BINS
    values = jnp.where(full_bins | (bin_index == top_bin), TOK_DEV, values)
    values = jnp.where(bin_index == low_bin, TOK_DEV // 4, values)
    return values.astype(jnp.int32)


def levels(key, shape, cuts, low, largest):
    def one(dim, shards_of):
        heights = jax.random.uniform(jax.random.fold_in(jax.random.fold_in(key, 6), dim), (shards_of,), jnp.float32, low / len(cuts), largest / len(cuts))
        return jnp.repeat(jnp.exp(heights), shape[dim] // shards_of).reshape((-1,) + (1,) * (len(shape) - dim - 1))

    level = one(*cuts[0])
    for cut in cuts[1:]:
        level = level * one(*cut)
    return level


def scatter_about(rng, shape, deviation, limit, cuts=(), held_as=jnp.bfloat16):
    loudness = levels(rng, shape, cuts, -0.22, 0.18) if cuts else 1.0
    entries = jax.random.normal(rng, shape, jnp.float32) * deviation * loudness
    return jnp.minimum(jnp.maximum(entries, -limit), limit).astype(held_as)


def setup_inputs(seed: int = 0) -> dict:
    arg_keys = jax.random.split(jax.random.key(seed), 6)
    hidden = draw_hidden(jax.random.fold_in(arg_keys[5], 71), 0)
    gain = jnp.clip(1.0 + 0.1 * jax.random.normal(arg_keys[1], (D,), jnp.float32), 0.5, 1.5)
    w_key = scatter_about(arg_keys[2], (D, KV * HD), 0.5, 3.0, ((1, 4),))
    grad_key = scatter_about(arg_keys[3], (TOKENS, KV * HD), 0.02, 0.119628906, ((0, 192), (1, 4)))
    counts = draw_counts(jax.random.fold_in(arg_keys[5], 71), 0)
    return dict(hidden=hidden, gain=gain, w_key=w_key, grad_key=grad_key, counts=counts)


EPSILON = 1e-05

def reference(hidden, gain, w_key, grad_key, counts):
    tokens, feature_width = hidden.shape
    bin_count = counts.shape[0]
    bin_tokens = tokens // bin_count
    real_total = jnp.sum(counts.astype(jnp.float32))
    weighting = jnp.float32(tokens) / real_total
    wide_hidden = hidden.astype(jnp.float32)
    inv_rms = lax.rsqrt(lax.optimization_barrier(jnp.mean(wide_hidden * wide_hidden, axis=1, keepdims=True)) + EPSILON)
    normed = (wide_hidden * inv_rms * gain).astype(jnp.bfloat16)
    position = jnp.arange(tokens) % bin_tokens
    bin_index = jnp.arange(tokens) // bin_tokens
    live_rows = position < counts[bin_index]
    masked_key = jnp.where(live_rows[:, None], grad_key, jnp.zeros((), jnp.bfloat16))
    summed_key = jnp.dot(normed.T, masked_key, preferred_element_type=jnp.float32)
    key_grad = jnp.pad(summed_key * weighting, ((0, D_PAD - D), (0, 0)))
    blocks = masked_key.reshape(bin_count, bin_tokens, KV * HD)

    def per_bin(bin_block):
        running = jnp.zeros((bin_tokens, feature_width), jnp.float32)
        for head_index in range(KV):
            head_slice = slice(head_index * HD, (head_index + 1) * HD)
            rounded = jnp.dot(bin_block[:, head_slice], w_key[:, head_slice].T, preferred_element_type=jnp.float32).astype(jnp.bfloat16)
            rounded = lax.optimization_barrier(rounded)
            running = running + rounded.astype(jnp.float32)
        return (running * weighting).astype(jnp.bfloat16)
    normed_grad = lax.map(per_bin, blocks).reshape(tokens, feature_width)
    return (key_grad, normed_grad)
```

```python
import functools

import jax
import jax.numpy as jnp
from jax import lax
from jax.experimental import pallas as pl
from jax.experimental.pallas import tpu as pltpu
from jax.sharding import Mesh
from jax.sharding import PartitionSpec as P

DP = ("dp_0", "dp_1", "dp_2")
MESH = pl.DeviceIdType.MESH
EPSILON = 1e-05
Z, Y, X = 12, 8, 4
TOK, D, HD = 128, 8192, 128
ROWS = 43
CHUNK = 16 * ROWS
HALF, LIFT = 352, 336
FAR, FAR_STEP = 112, 80
OWN = 64
NEAR = (3, 9, 2, 10, 1, 11)
FARS = (4, 5, 6, 7, 8)
SHARE = D // X


def own_start(block):
    return lax.div(ROWS * block, 16) * 16


def kernel(
    hid_hbm, w_hbm, gk_hbm, gain_ref, cnt_ref, kg_ref, ng_hbm,
    hid, wbuf, heads, part, pair, summed, near, far, near_sum, far_sum, near_in, far_in, acc, ngv,
    cnt_own, cnt_in, cnt_mid, cnt_in2,
    hid_sem, loc_sem, out_sem,
    wx_s, wx_r, gx_s, gx_r, wf_s, wf_r, pair_s, pair_r, near_s, near_r, far_s, far_r,
    n2_s, n2_r, f2_s, f2_r, c1_s, c1_r, c2_s, c2_r,
):
    z = lax.axis_index("dp_0")
    y = lax.axis_index("dp_1")
    c = lax.axis_index("dp_2")
    x = lax.axis_index("tensor")
    half = lax.div(y, 4)
    at_z = lambda d: lax.rem(z + d, Z)
    at_y = lambda d: lax.rem(y + d, Y)

    def remote(src, dst, ss, rs, zz=None, yy=None, cc=None, xx=None):
        return pltpu.make_async_remote_copy(
            src_ref=src, dst_ref=dst, send_sem=ss, recv_sem=rs,
            device_id=(
                z if zz is None else zz,
                y if yy is None else yy,
                c if cc is None else cc,
                x if xx is None else xx,
            ),
            device_id_type=MESH,
        )

    loads = []
    for i in range(4):
        cols = pl.ds(i * SHARE, SHARE)
        load = pltpu.make_async_copy(hid_hbm.at[:, cols], hid.at[:, cols], hid_sem.at[i])
        load.start()
        loads.append(load)
    gk_load = pltpu.make_async_copy(gk_hbm, heads.at[0], loc_sem.at[0])
    gk_load.start()
    mine = pl.ds(pl.multiple_of(x * SHARE, SHARE), SHARE)
    w_load = pltpu.make_async_copy(w_hbm.at[mine, :], wbuf.at[0], loc_sem.at[1])
    w_load.start()

    barrier = pltpu.get_barrier_semaphore()

    def greet(zz, yy, cc, xx):
        pl.semaphore_signal(barrier, inc=1, device_id=(zz, yy, cc, xx), device_id_type=MESH)

    greet(z, y, 1 - c, x)
    for k in range(1, X):
        greet(z, y, c, lax.rem(x + k, X))
    for d in range(1, Y):
        greet(z, at_y(d), c, x)
        greet(z, at_y(d), 1 - c, x)
    for d in range(1, Z):
        greet(at_z(d), y, c, x)
    for d in FARS:
        greet(at_z(d), y, 1 - c, x)
    greeted = 1 + 3 + 14 + 11 + 5

    count = cnt_ref[0]
    cnt_own[...] = jnp.full((8, 128), count, jnp.int32).astype(jnp.float32)

    squares = jnp.zeros((TOK, 128), jnp.float32)
    for i in range(4):
        loads[i].wait()

        def add_squares(t, total, i=i):
            lanes = pl.ds(pl.multiple_of(i * SHARE + t * 128, 128), 128)
            v = hid[:, lanes].astype(jnp.float32)
            return total + v * v

        squares = lax.fori_loop(0, SHARE // 128, add_squares, squares, unroll=4)
    inv_rms = lax.rsqrt(jnp.sum(squares, axis=1, keepdims=True) * (1.0 / D) + EPSILON)
    live = lax.broadcasted_iota(jnp.int32, (TOK, HD), 0) < count
    gk_load.wait()
    scaled = jnp.where(live, heads[0].astype(jnp.float32) * inv_rms, 0.0).astype(jnp.bfloat16)

    pl.semaphore_wait(barrier, greeted)

    gx, wx = [], []
    for k in (2, 1, 3):
        xx = lax.rem(x + k, X)
        send = remote(gk_hbm, heads.at[k], gx_s.at[k - 1], gx_r.at[k - 1], xx=xx)
        send.start()
        gx.append(send)
    upper = pl.ds(pl.multiple_of(c * (SHARE // 2), SHARE // 2), SHARE // 2)
    for k in (1, 3, 2):
        xx = lax.rem(x + k, X)
        theirs = pl.ds(pl.multiple_of(xx * SHARE + c * (SHARE // 2), SHARE // 2), SHARE // 2)
        send = remote(
            w_hbm.at[theirs, :], wbuf.at[k, upper, :], wx_s.at[k - 1], wx_r.at[k - 1], xx=xx
        )
        send.start()
        wx.append((k, send))
    c1 = []
    for d in range(Y):
        for e in range(2):
            if d + e == 0:
                continue
            slot = 2 * d + e - 1
            send = remote(
                cnt_own, cnt_in.at[slot], c1_s.at[slot], c1_r.at[slot],
                yy=at_y(d), cc=c if e == 0 else 1 - c,
            )
            send.start()
            c1.append(send)

    BLOCK = 512

    def block_term(t, _):
        at = pl.multiple_of(t * BLOCK, BLOCK)
        term = lax.dot_general(
            hid[:, pl.ds(at, BLOCK)], scaled, (((0,), (0,)), ((), ())),
            preferred_element_type=jnp.float32,
        )
        part[pl.ds(at, BLOCK), :] = term.astype(jnp.bfloat16)
        return 0

    lax.fori_loop(0, D // BLOCK, block_term, 0)
    part[D:, :] = jnp.zeros((Z * CHUNK - D, HD), jnp.bfloat16)

    order = NEAR[:2] + FARS + NEAR[2:] + (0,)
    pairs = {}
    for j in order:
        rows = pl.ds(pl.multiple_of(at_z(j) * CHUNK + (1 - c) * LIFT, 16), HALF)
        pairs[j] = remote(
            part.at[rows, :], pair.at[j], pair_s.at[j], pair_r.at[j], cc=1 - c
        )
        pairs[j].start()
    near_sends, far_sends = [], []
    for j in order:
        pairs[j].wait_recv()
        rows = pl.ds(pl.multiple_of(at_z(j) * CHUNK + c * LIFT, 16), HALF)
        summed[j] = (
            part[rows, :].astype(jnp.float32) + pair[j].astype(jnp.float32)
        ).astype(jnp.bfloat16)
        if j in NEAR:
            n = NEAR.index(j)
            send = remote(summed.at[j], near.at[n], near_s.at[n], near_r.at[n], zz=at_z(j))
            send.start()
            near_sends.append(send)
        if j == FARS[-1]:
            for r in (4, 3, 5, 2, 6, 1, 7):
                yy = at_y(r)
                window = pl.ds(pl.multiple_of(lax.rem(yy, 4) * FAR_STEP, 16), FAR)
                send = remote(
                    summed.at[pl.ds(FARS[0], len(FARS)), window, :], far.at[r - 1],
                    far_s.at[r - 1], far_r.at[r - 1], yy=yy,
                )
                there = lax.div(yy, 4) == c
                pl.when(there)(send.start)
                far_sends.append((there, send))

    for send in c1:
        send.wait_recv()
    cnt_mid[...] = cnt_own[...] + jnp.sum(cnt_in[...], axis=0)
    c2 = []
    for d in range(1, Z):
        send = remote(cnt_mid, cnt_in2.at[d - 1], c2_s.at[d - 1], c2_r.at[d - 1], zz=at_z(d))
        send.start()
        c2.append(send)

    wf = []
    for k, send in wx:
        send.wait_recv()
        forward = remote(
            wbuf.at[k, upper, :], wbuf.at[k, upper, :], wf_s.at[k - 1], wf_r.at[k - 1], cc=1 - c
        )
        forward.start()
        wf.append(forward)

    for send in near_sends:
        send.wait_recv()

    def near_total(t, _):
        rows = pl.ds(pl.multiple_of(t * 32, 32), 32)
        total = summed[0, rows, :].astype(jnp.float32)
        for n in range(len(NEAR)):
            total = total + near[n, rows, :].astype(jnp.float32)
        near_sum[rows, :] = total.astype(jnp.bfloat16)
        return 0

    lax.fori_loop(0, HALF // 32, near_total, 0)
    n2 = []
    for r in (4, 3, 5, 2, 6, 1, 7, 0):
        yy = at_y(r)
        for e in range(2):
            window = pl.ds(pl.multiple_of(own_start(2 * lax.rem(yy, 4) + e), 16), OWN)
            send = remote(
                near_sum.at[window, :], near_in.at[r], n2_s.at[2 * r + e], n2_r.at[r], yy=yy, cc=e
            )
            there = lax.div(yy, 4) == c
            if r == 0:
                there = jnp.logical_and(there, c != e)
            pl.when(there)(send.start)
            n2.append((there, send))
    mine8 = 2 * lax.rem(y, 4) + c

    @pl.when(half == c)
    def _():
        near_in[0] = near_sum[pl.ds(pl.multiple_of(own_start(mine8), 16), OWN), :]

    f2 = []
    quarter = lax.rem(y, 4)
    for n, j in enumerate(FARS):
        for e in range(2):
            inside = own_start(2 * quarter + e) - FAR_STEP * quarter
            window = pl.ds(pl.multiple_of(inside, 16), OWN)
            f2.append(
                remote(
                    far_sum.at[n, window, :], far_in.at[n], f2_s.at[2 * n + e], f2_r.at[n],
                    zz=at_z(j), cc=e,
                )
            )

    @pl.when(half == c)
    def _():
        for r in range(1, Y):
            pltpu.make_async_copy(far.at[r - 1], far.at[r - 1], far_r.at[r - 1]).wait()
        start = pl.multiple_of(quarter * FAR_STEP, 16)
        for n, j in enumerate(FARS):
            total = summed[j, pl.ds(start, FAR), :].astype(jnp.float32)
            for r in range(1, Y):
                total = total + far[r - 1, n].astype(jnp.float32)
            far_sum[n] = total.astype(jnp.bfloat16)
            for e in range(2):
                f2[2 * n + e].start()

    for send in c2:
        send.wait_recv()
    weighting = (1.0 * TOK * Z * Y * 2) / (cnt_mid[...] + jnp.sum(cnt_in2[...], axis=0))
    weight = weighting[0:1, 0:1]
    w_load.wait()
    for send in gx:
        send.wait_recv()
    for forward in wf:
        forward.wait_recv()
    for k in range(X):
        heads[k] = jnp.where(live, heads[k].astype(jnp.float32), 0.0).astype(jnp.bfloat16)
    TILE = 512
    outs = []
    for t in range(SHARE // TILE):
        cols = pl.ds(t * TILE, TILE)
        total = None
        for k in range(X):
            term = lax.dot_general(
                heads[k], wbuf[k, cols, :], (((1,), (1,)), ((), ())),
                preferred_element_type=jnp.float32,
            )
            total = term if total is None else total + term
        ngv[:, cols] = (total * weight).astype(jnp.bfloat16)
        out = pltpu.make_async_copy(ngv.at[:, cols], ng_hbm.at[:, cols], out_sem.at[t])
        out.start()
        outs.append(out)

    first = ROWS * ((z * Y + y) * 2 + c)
    shift = ROWS * mine8 + 8 * half - own_start(mine8)
    feature = first + lax.broadcasted_iota(jnp.int32, (48, 128), 0)
    lane = lax.broadcasted_iota(jnp.int32, (48, 128), 1)
    line = lax.div(first, 128)
    gains = jnp.zeros((48, 128), jnp.float32)
    for n in range(2):
        at = jnp.minimum(line + n, D // 128 - 1)
        row = gain_ref[pl.ds(at, 1), :]
        gains = jnp.where(feature == at * 128 + lane, row, gains)
    gain_rows = jnp.sum(gains, axis=1, keepdims=True)

    for r in range(1, Y):
        pltpu.make_async_copy(near_in.at[r], near_in.at[r], n2_r.at[r]).wait()

    @pl.when(half != c)
    def _():
        pltpu.make_async_copy(near_in.at[0], near_in.at[0], n2_r.at[0]).wait()

    for n in range(len(FARS)):
        pltpu.make_async_copy(far_in.at[n], far_in.at[n], f2_r.at[n]).wait()
    total = near_in[0].astype(jnp.float32)
    for r in range(1, Y):
        total = total + near_in[r].astype(jnp.float32)
    for n in range(len(FARS)):
        total = total + far_in[n].astype(jnp.float32)
    acc[0:OWN, :] = total
    own = acc[pl.ds(shift, 48), :] * (gain_rows * weight)
    kg_ref[...] = own[0:ROWS, :]

    for send in [*gx, *[s for _, s in wx], *c1, *wf, *pairs.values(), *near_sends, *c2]:
        send.wait_send()
    for there, send in [*far_sends, *n2]:
        pl.when(there)(send.wait_send)

    @pl.when(half == c)
    def _():
        for send in f2:
            send.wait_send()

    for out in outs:
        out.wait()


def fused(hidden, w_key, grad_key, gain, counts):
    bf16, f32 = jnp.bfloat16, jnp.float32
    dma = pltpu.SemaphoreType.DMA
    hbm = pl.BlockSpec(memory_space=pl.ANY)
    vmem = pl.BlockSpec(memory_space=pltpu.VMEM)
    return pl.pallas_call(
        kernel,
        out_shape=(
            jax.ShapeDtypeStruct((ROWS, HD), f32),
            jax.ShapeDtypeStruct((TOK, SHARE), bf16),
        ),
        in_specs=[hbm, hbm, hbm, vmem, pl.BlockSpec(memory_space=pltpu.SMEM)],
        out_specs=(vmem, hbm),
        scratch_shapes=[
            pltpu.VMEM((TOK, D), bf16),
            pltpu.VMEM((X, SHARE, HD), bf16),
            pltpu.VMEM((X, TOK, HD), bf16),
            pltpu.VMEM((Z * CHUNK, HD), bf16),
            pltpu.VMEM((Z, HALF, HD), bf16),
            pltpu.VMEM((Z, HALF, HD), bf16),
            pltpu.VMEM((len(NEAR), HALF, HD), bf16),
            pltpu.VMEM((Y - 1, len(FARS), FAR, HD), bf16),
            pltpu.VMEM((HALF, HD), bf16),
            pltpu.VMEM((len(FARS), FAR, HD), bf16),
            pltpu.VMEM((Y, OWN, HD), bf16),
            pltpu.VMEM((len(FARS), OWN, HD), bf16),
            pltpu.VMEM((OWN + 16, HD), f32),
            pltpu.VMEM((TOK, SHARE), bf16),
            pltpu.VMEM((8, 128), f32),
            pltpu.VMEM((15, 8, 128), f32),
            pltpu.VMEM((8, 128), f32),
            pltpu.VMEM((11, 8, 128), f32),
            dma((4,)), dma((2,)), dma((4,)),
            dma((3,)), dma((3,)), dma((3,)), dma((3,)), dma((3,)), dma((3,)),
            dma((Z,)), dma((Z,)), dma((6,)), dma((6,)), dma((7,)), dma((7,)),
            dma((16,)), dma((8,)), dma((10,)), dma((5,)), dma((15,)), dma((15,)),
            dma((11,)), dma((11,)),
        ],
        compiler_params=pltpu.CompilerParams(collective_id=0, has_side_effects=True),
    )(hidden, w_key, grad_key, gain, counts)


def per_device(hidden, gain, w_key, grad_key, counts):
    return fused(hidden, w_key, grad_key, gain.reshape(D // 128, 128), counts)


def solution(mesh):
    split = Mesh(
        mesh.devices.reshape(Z, Y, 2, mesh.shape["tensor"]), ("dp_0", "dp_1", "dp_2", "tensor")
    )
    return jax.shard_map(
        per_device,
        mesh=split,
        in_specs=(P(DP, None), P(), P(None, "tensor"), P(DP, "tensor"), P(DP)),
        out_specs=(P(DP, "tensor"), P(DP, "tensor")),
        check_vma=False,
    )
```

```python
import functools

import jax
import jax.numpy as jnp
from jax import lax
from jax.experimental import pallas as pl
from jax.experimental.pallas import tpu as pltpu
from jax.sharding import Mesh
from jax.sharding import PartitionSpec as P

DP = ("dp_0", "dp_1", "dp_2")
MESH = pl.DeviceIdType.MESH
EPSILON = 1e-05
Z, Y, X = 12, 8, 4
TOK, D, HD = 128, 8192, 128
ROWS = 43
CHUNK = 16 * ROWS
HALF, LIFT = 352, 336
FAR, FAR_STEP = 112, 80
OWN = 64
NEAR = (3, 9, 2, 10, 1, 11)
FARS = (4, 5, 6, 7, 8)
SHARE = D // X


def own_start(block):
    return lax.div(ROWS * block, 16) * 16


def kernel(
    hid_hbm, w_hbm, gk_hbm, gain_hbm, cnt_hbm, kg_ref, ng_hbm,
    gain_ref, cnt_ref, hid, turned, wbuf, heads, part, pair, summed, near, far, near_sum, far_sum, near_in, far_in, acc, ngv,
    cnt_own, cnt_in, cnt_mid, cnt_in2,
    hid_sem, loc_sem, out_sem,
    wx_s, wx_r, gx_s, gx_r, wf_s, wf_r, pair_s, pair_r, near_s, near_r, far_s, far_r,
    n2_s, n2_r, f2_s, f2_r, c1_s, c1_r, c2_s, c2_r,
):
    z = lax.axis_index("dp_0")
    y = lax.axis_index("dp_1")
    c = lax.axis_index("dp_2")
    x = lax.axis_index("tensor")
    half = lax.div(y, 4)
    at_z = lambda d: lax.rem(z + d, Z)
    at_y = lambda d: lax.rem(y + d, Y)

    def remote(src, dst, ss, rs, zz=None, yy=None, cc=None, xx=None):
        return pltpu.make_async_remote_copy(
            src_ref=src, dst_ref=dst, send_sem=ss, recv_sem=rs,
            device_id=(
                z if zz is None else zz,
                y if yy is None else yy,
                c if cc is None else cc,
                x if xx is None else xx,
            ),
            device_id_type=MESH,
        )

    loads = []
    for i in range(4):
        cols = pl.ds(i * SHARE, SHARE)
        load = pltpu.make_async_copy(hid_hbm.at[:, cols], hid.at[:, cols], hid_sem.at[i])
        load.start()
        loads.append(load)
    gk_load = pltpu.make_async_copy(gk_hbm, heads.at[0], loc_sem.at[0])
    gk_load.start()
    cnt_load = pltpu.make_async_copy(cnt_hbm, cnt_ref, loc_sem.at[2])
    cnt_load.start()
    gain_load = pltpu.make_async_copy(gain_hbm, gain_ref, loc_sem.at[3])
    gain_load.start()
    mine = pl.ds(pl.multiple_of(x * SHARE, SHARE), SHARE)
    w_load = pltpu.make_async_copy(w_hbm.at[mine, :], wbuf.at[0], loc_sem.at[1])
    w_load.start()

    barrier = pltpu.get_barrier_semaphore()

    def greet(zz, yy, cc, xx):
        pl.semaphore_signal(barrier, inc=1, device_id=(zz, yy, cc, xx), device_id_type=MESH)

    greet(z, y, 1 - c, x)
    for k in range(1, X):
        greet(z, y, c, lax.rem(x + k, X))
    for d in range(1, Y):
        greet(z, at_y(d), c, x)
        greet(z, at_y(d), 1 - c, x)
    for d in range(1, Z):
        greet(at_z(d), y, c, x)
    for d in FARS:
        greet(at_z(d), y, 1 - c, x)
    greeted = 1 + 3 + 14 + 11 + 5

    cnt_load.wait()
    count = cnt_ref[0]
    cnt_own[...] = jnp.full((8, 128), count, jnp.int32).astype(jnp.float32)

    squares = jnp.zeros((TOK, 128), jnp.float32)
    for i in range(4):
        loads[i].wait()

        def add_squares(t, total, i=i):
            lanes = pl.ds(pl.multiple_of(i * SHARE + t * 128, 128), 128)
            block = hid[:, lanes]
            turned[lanes, :] = block.T
            v = block.astype(jnp.float32)
            return total + v * v

        squares = lax.fori_loop(0, SHARE // 128, add_squares, squares, unroll=4)
    inv_rms = lax.rsqrt(jnp.sum(squares, axis=1, keepdims=True) * (1.0 / D) + EPSILON)
    live = lax.broadcasted_iota(jnp.int32, (TOK, HD), 0) < count
    gk_load.wait()
    scaled = jnp.where(live, heads[0].astype(jnp.float32) * inv_rms, 0.0).astype(jnp.bfloat16)

    BLOCK = 512

    def block_term(t, _):
        at = pl.multiple_of(t * BLOCK, BLOCK)
        term = jnp.dot(turned[pl.ds(at, BLOCK), :], scaled, preferred_element_type=jnp.float32)
        part[pl.ds(at, BLOCK), :] = term.astype(jnp.bfloat16)
        return 0

    lax.fori_loop(0, D // BLOCK, block_term, 0, unroll=2)
    part[D:, :] = jnp.zeros((Z * CHUNK - D, HD), jnp.bfloat16)

    pl.semaphore_wait(barrier, greeted)

    gx, wx = [], []
    for k in (2, 1, 3):
        xx = lax.rem(x + k, X)
        send = remote(gk_hbm, heads.at[k], gx_s.at[k - 1], gx_r.at[k - 1], xx=xx)
        send.start()
        gx.append(send)
    upper = pl.ds(pl.multiple_of(c * (SHARE // 2), SHARE // 2), SHARE // 2)
    for k in (1, 3, 2):
        xx = lax.rem(x + k, X)
        theirs = pl.ds(pl.multiple_of(xx * SHARE + c * (SHARE // 2), SHARE // 2), SHARE // 2)
        send = remote(
            w_hbm.at[theirs, :], wbuf.at[k, upper, :], wx_s.at[k - 1], wx_r.at[k - 1], xx=xx
        )
        send.start()
        wx.append((k, send))
    c1 = []
    for d in range(Y):
        for e in range(2):
            if d + e == 0:
                continue
            slot = 2 * d + e - 1
            send = remote(
                cnt_own, cnt_in.at[slot], c1_s.at[slot], c1_r.at[slot],
                yy=at_y(d), cc=c if e == 0 else 1 - c,
            )
            send.start()
            c1.append(send)

    order = NEAR[:2] + FARS + NEAR[2:] + (0,)
    pairs = {}
    for j in order:
        rows = pl.ds(pl.multiple_of(at_z(j) * CHUNK + (1 - c) * LIFT, 16), HALF)
        pairs[j] = remote(
            part.at[rows, :], pair.at[j], pair_s.at[j], pair_r.at[j], cc=1 - c
        )
        pairs[j].start()
    near_sends, far_sends = [], []
    for j in order:
        pairs[j].wait_recv()
        rows = pl.ds(pl.multiple_of(at_z(j) * CHUNK + c * LIFT, 16), HALF)
        summed[j] = (
            part[rows, :].astype(jnp.float32) + pair[j].astype(jnp.float32)
        ).astype(jnp.bfloat16)
        if j in NEAR:
            n = NEAR.index(j)
            send = remote(summed.at[j], near.at[n], near_s.at[n], near_r.at[n], zz=at_z(j))
            send.start()
            near_sends.append(send)
        if j == FARS[-1]:
            for r in (4, 3, 5, 2, 6, 1, 7):
                yy = at_y(r)
                window = pl.ds(pl.multiple_of(lax.rem(yy, 4) * FAR_STEP, 16), FAR)
                send = remote(
                    summed.at[pl.ds(FARS[0], len(FARS)), window, :], far.at[r - 1],
                    far_s.at[r - 1], far_r.at[r - 1], yy=yy,
                )
                there = lax.div(yy, 4) == c
                pl.when(there)(send.start)
                far_sends.append((there, send))

    for send in c1:
        send.wait_recv()
    cnt_mid[...] = cnt_own[...] + jnp.sum(cnt_in[...], axis=0)
    c2 = []
    for d in range(1, Z):
        send = remote(cnt_mid, cnt_in2.at[d - 1], c2_s.at[d - 1], c2_r.at[d - 1], zz=at_z(d))
        send.start()
        c2.append(send)

    wf = []
    for k, send in wx:
        send.wait_recv()
        forward = remote(
            wbuf.at[k, upper, :], wbuf.at[k, upper, :], wf_s.at[k - 1], wf_r.at[k - 1], cc=1 - c
        )
        forward.start()
        wf.append(forward)

    for send in near_sends:
        send.wait_recv()

    def near_total(t, _):
        rows = pl.ds(pl.multiple_of(t * 32, 32), 32)
        total = summed[0, rows, :].astype(jnp.float32)
        for n in range(len(NEAR)):
            total = total + near[n, rows, :].astype(jnp.float32)
        near_sum[rows, :] = total.astype(jnp.bfloat16)
        return 0

    lax.fori_loop(0, HALF // 32, near_total, 0)
    n2 = []
    for r in (4, 3, 5, 2, 6, 1, 7, 0):
        yy = at_y(r)
        for e in range(2):
            window = pl.ds(pl.multiple_of(own_start(2 * lax.rem(yy, 4) + e), 16), OWN)
            send = remote(
                near_sum.at[window, :], near_in.at[r], n2_s.at[2 * r + e], n2_r.at[r], yy=yy, cc=e
            )
            there = lax.div(yy, 4) == c
            if r == 0:
                there = jnp.logical_and(there, c != e)
            pl.when(there)(send.start)
            n2.append((there, send))
    mine8 = 2 * lax.rem(y, 4) + c

    @pl.when(half == c)
    def _():
        near_in[0] = near_sum[pl.ds(pl.multiple_of(own_start(mine8), 16), OWN), :]

    f2 = []
    quarter = lax.rem(y, 4)
    for n, j in enumerate(FARS):
        for e in range(2):
            inside = own_start(2 * quarter + e) - FAR_STEP * quarter
            window = pl.ds(pl.multiple_of(inside, 16), OWN)
            f2.append(
                remote(
                    far_sum.at[n, window, :], far_in.at[n], f2_s.at[2 * n + e], f2_r.at[n],
                    zz=at_z(j), cc=e,
                )
            )

    @pl.when(half == c)
    def _():
        for r in range(1, Y):
            pltpu.make_async_copy(far.at[r - 1], far.at[r - 1], far_r.at[r - 1]).wait()
        start = pl.multiple_of(quarter * FAR_STEP, 16)
        for n, j in enumerate(FARS):
            total = summed[j, pl.ds(start, FAR), :].astype(jnp.float32)
            for r in range(1, Y):
                total = total + far[r - 1, n].astype(jnp.float32)
            far_sum[n] = total.astype(jnp.bfloat16)
            for e in range(2):
                f2[2 * n + e].start()

    for send in c2:
        send.wait_recv()
    weighting = (1.0 * TOK * Z * Y * 2) / (cnt_mid[...] + jnp.sum(cnt_in2[...], axis=0))
    weight = weighting[0:1, 0:1]
    w_load.wait()
    for send in gx:
        send.wait_recv()
    for forward in wf:
        forward.wait_recv()
    for k in range(X):
        heads[k] = jnp.where(live, heads[k].astype(jnp.float32), 0.0).astype(jnp.bfloat16)
    TILE = 512
    outs = []
    for t in range(SHARE // TILE):
        cols = pl.ds(t * TILE, TILE)
        total = None
        for k in range(X):
            term = lax.dot_general(
                heads[k], wbuf[k, cols, :], (((1,), (1,)), ((), ())),
                preferred_element_type=jnp.float32,
            )
            total = term if total is None else total + term
        ngv[:, cols] = (total * weight).astype(jnp.bfloat16)
        out = pltpu.make_async_copy(ngv.at[:, cols], ng_hbm.at[:, cols], out_sem.at[t])
        out.start()
        outs.append(out)

    gain_load.wait()
    first = ROWS * ((z * Y + y) * 2 + c)
    shift = ROWS * mine8 + 8 * half - own_start(mine8)
    feature = first + lax.broadcasted_iota(jnp.int32, (48, 128), 0)
    lane = lax.broadcasted_iota(jnp.int32, (48, 128), 1)
    line = lax.div(first, 128)
    gains = jnp.zeros((48, 128), jnp.float32)
    for n in range(2):
        at = jnp.minimum(line + n, D // 128 - 1)
        row = gain_ref[pl.ds(at, 1), :]
        gains = jnp.where(feature == at * 128 + lane, row, gains)
    gain_rows = jnp.sum(gains, axis=1, keepdims=True)

    for r in range(1, Y):
        pltpu.make_async_copy(near_in.at[r], near_in.at[r], n2_r.at[r]).wait()

    @pl.when(half != c)
    def _():
        pltpu.make_async_copy(near_in.at[0], near_in.at[0], n2_r.at[0]).wait()

    for n in range(len(FARS)):
        pltpu.make_async_copy(far_in.at[n], far_in.at[n], f2_r.at[n]).wait()
    total = near_in[0].astype(jnp.float32)
    for r in range(1, Y):
        total = total + near_in[r].astype(jnp.float32)
    for n in range(len(FARS)):
        total = total + far_in[n].astype(jnp.float32)
    acc[0:OWN, :] = total
    own = acc[pl.ds(shift, 48), :] * (gain_rows * weight)
    kg_ref[...] = own[0:ROWS, :]

    for send in [*gx, *[s for _, s in wx], *c1, *wf, *pairs.values(), *near_sends, *c2]:
        send.wait_send()
    for there, send in [*far_sends, *n2]:
        pl.when(there)(send.wait_send)

    @pl.when(half == c)
    def _():
        for send in f2:
            send.wait_send()

    for out in outs:
        out.wait()


def fused(hidden, w_key, grad_key, gain, counts):
    bf16, f32 = jnp.bfloat16, jnp.float32
    dma = pltpu.SemaphoreType.DMA
    hbm = pl.BlockSpec(memory_space=pltpu.HBM)
    anywhere = pl.BlockSpec(memory_space=pl.ANY)
    vmem = pl.BlockSpec(memory_space=pltpu.VMEM)
    return pl.pallas_call(
        kernel,
        out_shape=(
            jax.ShapeDtypeStruct((ROWS, HD), f32),
            jax.ShapeDtypeStruct((TOK, SHARE), bf16),
        ),
        in_specs=[hbm] * 5,
        out_specs=(vmem, anywhere),
        scratch_shapes=[
            pltpu.VMEM((D // 128, 128), f32),
            pltpu.SMEM((1,), jnp.int32),
            pltpu.VMEM((TOK, D), bf16),
            pltpu.VMEM((D, TOK), bf16),
            pltpu.VMEM((X, SHARE, HD), bf16),
            pltpu.VMEM((X, TOK, HD), bf16),
            pltpu.VMEM((Z * CHUNK, HD), bf16),
            pltpu.VMEM((Z, HALF, HD), bf16),
            pltpu.VMEM((Z, HALF, HD), bf16),
            pltpu.VMEM((len(NEAR), HALF, HD), bf16),
            pltpu.VMEM((Y - 1, len(FARS), FAR, HD), bf16),
            pltpu.VMEM((HALF, HD), bf16),
            pltpu.VMEM((len(FARS), FAR, HD), bf16),
            pltpu.VMEM((Y, OWN, HD), bf16),
            pltpu.VMEM((len(FARS), OWN, HD), bf16),
            pltpu.VMEM((OWN + 16, HD), f32),
            pltpu.VMEM((TOK, SHARE), bf16),
            pltpu.VMEM((8, 128), f32),
            pltpu.VMEM((15, 8, 128), f32),
            pltpu.VMEM((8, 128), f32),
            pltpu.VMEM((11, 8, 128), f32),
            dma((4,)), dma((4,)), dma((4,)),
            dma((3,)), dma((3,)), dma((3,)), dma((3,)), dma((3,)), dma((3,)),
            dma((Z,)), dma((Z,)), dma((6,)), dma((6,)), dma((7,)), dma((7,)),
            dma((16,)), dma((8,)), dma((10,)), dma((5,)), dma((15,)), dma((15,)),
            dma((11,)), dma((11,)),
        ],
        compiler_params=pltpu.CompilerParams(collective_id=0, has_side_effects=True, vmem_limit_bytes=24 << 20),
    )(hidden, w_key, grad_key, gain, counts)


def per_device(hidden, gain, w_key, grad_key, counts):
    in_hbm = lambda v: pltpu.with_memory_space_constraint(v, pltpu.HBM)
    gain = gain.reshape(D // 128, 128)
    return fused(*(in_hbm(v) for v in (hidden, w_key, grad_key, gain)), counts)


def solution(mesh):
    split = Mesh(
        mesh.devices.reshape(Z, Y, 2, mesh.shape["tensor"]), ("dp_0", "dp_1", "dp_2", "tensor")
    )
    return jax.shard_map(
        per_device,
        mesh=split,
        in_specs=(P(DP, None), P(), P(None, "tensor"), P(DP, "tensor"), P(DP)),
        out_specs=(P(DP, "tensor"), P(DP, "tensor")),
        check_vma=False,
    )
```

```python
import jax
import jax.numpy as jnp
from jax import lax
from jax.experimental import pallas as pl
from jax.experimental.pallas import tpu as pltpu
from jax.sharding import Mesh
from jax.sharding import PartitionSpec as P

DP = ("dp_0", "dp_1", "dp_2")
MESH = pl.DeviceIdType.MESH
EPSILON = 1e-05
Z, Y, X = 12, 8, 4
TOK, D, HD = 128, 8192, 128
ROWS = 43
CHUNK = 16 * ROWS
HALF, LIFT = 352, 336
LEAD = 4
FAR = 96
OWN = 48
FARS = (6, 5, 7, 4, 8)
PARTS = ((0, 2, 1), (2, 5, -1))
GROUPS = (FARS[:2], FARS[2:], (3, 9), (1, 11, 2, 10, 0))
NF = len(FARS)
SHARE = D // X


def kernel(
    hid_hbm, w_hbm, gk_hbm, gain_hbm, cnt_hbm, kg_ref, ng_hbm,
    gain_ref, cnt_ref, hid, turned, wbuf, heads, scaled, other, pair, shifted, summed, sumfar,
    near_mid, near_out, near, far_mid, far_out, far,
    near_f, near_own, far_f, far_own, near_in, far_in, ngv,
    cnt_own, cnt_in, cnt_mid, cnt_in2,
    hid_sem, loc_sem, out_sem,
    wx_s, wx_r, gx_s, gx_r, wf_s, wf_r, pair_s, pair_r, near_s, near_r, far_s, far_r,
    n2_s, n2_r, f2_s, f2_r, c1_s, c1_r, c2_s, c2_r,
):
    z = lax.axis_index("dp_0")
    y = lax.axis_index("dp_1")
    c = lax.axis_index("dp_2")
    x = lax.axis_index("tensor")
    half, quarter = lax.div(y, 4), lax.rem(y, 4)
    at_z = lambda d: lax.rem(z + d, Z)
    at_y = lambda d: lax.rem(y + d, Y)
    f32, bf16 = jnp.float32, jnp.bfloat16

    def remote(src, dst, ss, rs, zz=None, yy=None, cc=None, xx=None):
        return pltpu.make_async_remote_copy(
            src_ref=src, dst_ref=dst, send_sem=ss, recv_sem=rs,
            device_id=(
                z if zz is None else zz,
                y if yy is None else yy,
                c if cc is None else cc,
                x if xx is None else xx,
            ),
            device_id_type=MESH,
        )

    PIECES = 8
    loads = []
    for i in range(PIECES):
        cols = pl.ds(i * (D // PIECES), D // PIECES)
        load = pltpu.make_async_copy(hid_hbm.at[:, cols], hid.at[:, cols], hid_sem.at[i])
        load.start()
        loads.append(load)
    cnt_load = pltpu.make_async_copy(cnt_hbm, cnt_ref, loc_sem.at[2])
    cnt_load.start()
    gk_load = pltpu.make_async_copy(gk_hbm, heads.at[0], loc_sem.at[0])
    gk_load.start()
    gain_load = pltpu.make_async_copy(gain_hbm, gain_ref, loc_sem.at[3])
    gain_load.start()
    mine = pl.ds(pl.multiple_of(x * SHARE, SHARE), SHARE)
    w_load = pltpu.make_async_copy(w_hbm.at[mine, :], wbuf.at[0], loc_sem.at[1])
    w_load.start()

    barrier = pltpu.get_barrier_semaphore()

    def greet(zz, yy, cc, xx):
        pl.semaphore_signal(barrier, inc=1, device_id=(zz, yy, cc, xx), device_id_type=MESH)

    for d in (6, 5, 7, 4, 8, 3, 9, 2, 10, 1, 11):
        greet(at_z(d), y, c, x)
        if d in FARS:
            greet(at_z(d), y, 1 - c, x)
    for d in (4, 3, 5, 2, 6, 1, 7):
        greet(z, at_y(d), c, x)
        greet(z, at_y(d), 1 - c, x)
    for k in range(1, X):
        greet(z, y, c, lax.rem(x + k, X))
    greet(z, y, 1 - c, x)
    greeted = 1 + 3 + 14 + 11 + NF

    cnt_load.wait()
    count = cnt_ref[0]
    cnt_own[...] = jnp.full((8, 128), count, jnp.int32).astype(f32)
    turned[D:, :] = jnp.zeros((Z * CHUNK - D, TOK), bf16)
    for s in range(NF):
        shifted[s, 0:8, :] = jnp.zeros((8, 128), f32)
        shifted[s, HALF + 8 :, :] = jnp.zeros((8, 128), f32)

    squares = jnp.zeros((TOK, 128), f32)
    for i in range(PIECES):
        loads[i].wait()

        def add_squares(t, total, i=i):
            lanes = pl.ds(pl.multiple_of(i * (D // PIECES) + t * 128, 128), 128)
            block = hid[:, lanes]
            turned[lanes, :] = block.T
            v = block.astype(f32)
            return total + v * v

        squares = lax.fori_loop(0, D // PIECES // 128, add_squares, squares, unroll=4)
    inv_rms = lax.rsqrt(jnp.sum(squares, axis=1, keepdims=True) * (1.0 / D) + EPSILON)
    live = lax.broadcasted_iota(jnp.int32, (TOK, HD), 0) < count
    gk_load.wait()
    scaled[...] = jnp.where(live, heads[0].astype(f32) * inv_rms, 0.0).astype(bf16)

    pl.semaphore_wait(barrier, greeted)

    near_sends, far_sends = {}, []
    pairs, gx, wx, c1 = {}, [], [], []
    upper = pl.ds(pl.multiple_of(c * (SHARE // 2), SHARE // 2), SHARE // 2)

    def window(target):
        start = lax.div(LEAD + 2 * ROWS * lax.rem(target, 4), 16) * 16
        return pl.ds(pl.multiple_of(start, 16), FAR)

    def here(r):
        return lax.div(at_y(r), 4) == c

    def mine_far(r, first, last):
        return sumfar.at[pl.ds(first, last - first), window(at_y(r)), :]

    def share(j):
        theirs = pl.multiple_of(at_z(j) * CHUNK + (1 - c) * LIFT, 16)
        pairs[j] = remote(
            turned.at[pl.ds(theirs, HALF), :], pair.at[j], pair_s.at[j], pair_r.at[j], cc=1 - c
        )
        pairs[j].start()

    def weights_along_x():
        for k in (1, 3, 2):
            xx = lax.rem(x + k, X)
            theirs = pl.ds(pl.multiple_of(xx * SHARE + c * (SHARE // 2), SHARE // 2), SHARE // 2)
            send = remote(
                w_hbm.at[theirs, :], wbuf.at[k, upper, :], wx_s.at[k - 1], wx_r.at[k - 1], xx=xx
            )
            send.start()
            wx.append((k, send))
        for k in (2, 1, 3):
            xx = lax.rem(x + k, X)
            send = remote(gk_hbm, heads.at[k], gx_s.at[k - 1], gx_r.at[k - 1], xx=xx)
            send.start()
            gx.append(send)

    def counts_along_y():
        for d in range(Y):
            for e in range(2):
                if d + e == 0:
                    continue
                slot = 2 * d + e - 1
                send = remote(
                    cnt_own, cnt_in.at[slot], c1_s.at[slot], c1_r.at[slot],
                    yy=at_y(d), cc=c if e == 0 else 1 - c,
                )
                send.start()
                c1.append(send)

    def send_near(i, src, dst, step):
        near_sends[i] = remote(src, dst, near_s.at[i], near_r.at[i], zz=at_z(step))
        near_sends[i].start()

    def send_far(i, src, dst, r, step):
        send = remote(src, dst, far_s.at[i], far_r.at[i], yy=at_y(step))
        pl.when(here(r))(send.start)
        far_sends.append((here(r), send))

    def finish(group, both):
        tokens = []
        for j in group:
            pairs[j].wait_recv()
            rows = pl.ds(pl.multiple_of(at_z(j) * CHUNK + c * LIFT, 16), HALF)
            tokens.append(jnp.concatenate([turned[rows, :], pair[j]], axis=1))
        total = jnp.dot(jnp.concatenate(tokens, axis=0), both, preferred_element_type=f32)
        for n, j in enumerate(group):
            one = total[n * HALF : (n + 1) * HALF]
            if j in FARS:
                i = FARS.index(j)
                shifted[i, 8 : HALF + 8, :] = one
                sumfar[i] = shifted[i, pl.ds(8 - LEAD + 8 * c, HALF), :].astype(bf16)
            else:
                summed[j] = one.astype(bf16)

    swap = remote(scaled, other, pair_s.at[Z], pair_r.at[Z], cc=1 - c)
    swap.start()
    pairs[Z] = swap
    for group in GROUPS:
        for j in group:
            share(j)
    weights_along_x()
    counts_along_y()
    swap.wait_recv()
    both = jnp.concatenate([scaled[...], other[...]], axis=0)
    def first_far(p):
        first, last, way = PARTS[p]
        n = pl.ds(first, last - first)
        for i, (r, dst, step) in enumerate(
            (
                (4, far_mid.at[0, n], way),
                (-3 * way, far_mid.at[1, n], -way),
                (2 * way, far_mid.at[2, n], way),
                (-way, far.at[0, n], -way),
            )
        ):
            send_far(7 * p + i, mine_far(r % Y, first, last), dst, r % Y, step % Y)

    finish(GROUPS[0], both)
    first_far(0)
    finish(GROUPS[1], both)
    first_far(1)
    finish(GROUPS[2], both)
    send_near(0, summed.at[3], near_mid.at[0], 1)
    send_near(1, summed.at[9], near_mid.at[1], 11)
    finish(GROUPS[3], both)
    send_near(2, summed.at[1], near.at[0], 1)
    send_near(3, summed.at[11], near.at[1], 11)

    for p, (first, last, way) in enumerate(PARTS):
        n = pl.ds(first, last - first)
        for m, r in enumerate((3 * way % Y, -2 * way % Y, way % Y)):

            @pl.when(here(r))
            def _(p=p, n=n, m=m, r=r, first=first, last=last):
                mid = far_mid.at[m, n]
                pltpu.make_async_copy(mid, mid, far_r.at[7 * p + m]).wait()
                rows = window(at_y(r))
                for i in range(first, last):
                    far_out[m, i] = sumfar[i, rows, :] + far_mid[m, i]

            send_far(7 * p + 4 + m, far_out.at[m, n], far.at[1 + m, n], r, r)

    for n, (j, step) in enumerate(((2, 2), (10, 10))):
        near_sends[n].wait_recv()

        def merge_near(t, _, n=n, j=j):
            rows = pl.ds(pl.multiple_of(t * 32, 32), 32)
            near_out[n, rows, :] = summed[j, rows, :] + near_mid[n, rows, :]
            return 0

        lax.fori_loop(0, HALF // 32, merge_near, 0, unroll=True)
        send_near(4 + n, near_out.at[n], near.at[2 + n], step)

    for send in c1:
        send.wait_recv()
    cnt_mid[...] = cnt_own[...] + jnp.sum(cnt_in[...], axis=0)
    c2 = []
    for d in range(1, Z):
        send = remote(cnt_mid, cnt_in2.at[d - 1], c2_s.at[d - 1], c2_r.at[d - 1], zz=at_z(d))
        send.start()
        c2.append(send)

    f2 = []
    for i, j in enumerate(FARS):
        for e in range(2):
            f2.append(
                remote(
                    far_own.at[i, e], far_in.at[i], f2_s.at[2 * i + e], f2_r.at[i],
                    zz=at_z(j), cc=e,
                )
            )

    @pl.when(half == c)
    def _():
        rows = window(y)
        start = LEAD + 2 * ROWS * quarter
        inside = start - lax.div(start, 16) * 16
        for p, (first, last, way) in enumerate(PARTS):
            n = pl.ds(first, last - first)
            for slot in range(4):
                come = far.at[slot, n]
                pltpu.make_async_copy(come, come, far_r.at[7 * p + 3 + slot]).wait()
            for i in range(first, last):
                total = sumfar[i, rows, :].astype(f32)
                for slot in range(4):
                    total = total + far[slot, i].astype(f32)
                far_f[i, 0:FAR, :] = total
                for e in range(2):
                    far_own[i, e] = far_f[i, pl.ds(inside + e * ROWS, OWN), :].astype(bf16)
                    f2[2 * i + e].start()

    for i in (2, 3, 4, 5):
        near_sends[i].wait_recv()

    def near_total(t, _):
        rows = pl.ds(pl.multiple_of(t * 32, 32), 32)
        total = summed[0, rows, :].astype(f32)
        for n in range(4):
            total = total + near[n, rows, :].astype(f32)
        near_f[rows, :] = total
        return 0

    lax.fori_loop(0, HALF // 32, near_total, 0, unroll=True)
    for b in range(8):
        near_own[b] = near_f[pl.ds(8 * c + ROWS * b, OWN), :].astype(bf16)
    n2 = []
    for r in (4, 3, 5, 2, 6, 1, 7, 0):
        yy = at_y(r)
        for e in range(2):
            send = remote(
                near_own.at[2 * lax.rem(yy, 4) + e], near_in.at[r], n2_s.at[2 * r + e],
                n2_r.at[r], yy=yy, cc=e,
            )
            there = here(r)
            if r == 0:
                there = jnp.logical_and(there, c != e)
            pl.when(there)(send.start)
            n2.append((there, send))

    @pl.when(half == c)
    def _():
        near_in[0] = near_own[2 * quarter + c]

    wf = []
    for k, send in wx:
        send.wait_recv()
        forward = remote(
            wbuf.at[k, upper, :], wbuf.at[k, upper, :], wf_s.at[k - 1], wf_r.at[k - 1], cc=1 - c
        )
        forward.start()
        wf.append(forward)

    gain_load.wait()
    first = ROWS * ((z * Y + y) * 2 + c)
    feature = first + lax.broadcasted_iota(jnp.int32, (OWN, 128), 0)
    lane = lax.broadcasted_iota(jnp.int32, (OWN, 128), 1)
    line = lax.div(first, 128)
    gains = jnp.zeros((OWN, 128), f32)
    for n in range(2):
        at = jnp.minimum(line + n, D // 128 - 1)
        row = gain_ref[pl.ds(at, 1), :]
        gains = jnp.where(feature == at * 128 + lane, row, gains)
    gain_rows = jnp.sum(gains, axis=1, keepdims=True)

    w_load.wait()
    for send in gx:
        send.wait_recv()
    for k in range(X):
        heads[k] = jnp.where(live, heads[k].astype(f32), 0.0).astype(bf16)
    for send in c2:
        send.wait_recv()
    weighting = (1.0 * TOK * Z * Y * 2) / (cnt_mid[...] + jnp.sum(cnt_in2[...], axis=0))
    weight = weighting[0:1, 0:1]
    TILE = 512
    outs = []
    for t in range(SHARE // TILE):
        if 2 * t == SHARE // TILE:
            for forward in wf:
                forward.wait_recv()
        first_half = 2 * t < SHARE // TILE
        base = (c if first_half else 1 - c) * (SHARE // 2) + (t % (SHARE // TILE // 2)) * TILE
        cols = pl.ds(pl.multiple_of(base, TILE), TILE)
        total = None
        for k in range(X):
            term = lax.dot_general(
                heads[k], wbuf[k, cols, :], (((1,), (1,)), ((), ())),
                preferred_element_type=f32,
            )
            total = term if total is None else total + term
        ngv[:, cols] = (total * weight).astype(bf16)
        out = pltpu.make_async_copy(ngv.at[:, cols], ng_hbm.at[:, cols], out_sem.at[t])
        out.start()
        outs.append(out)

    for r in range(1, Y):
        pltpu.make_async_copy(near_in.at[r], near_in.at[r], n2_r.at[r]).wait()

    @pl.when(half != c)
    def _():
        pltpu.make_async_copy(near_in.at[0], near_in.at[0], n2_r.at[0]).wait()

    total = near_in[0].astype(f32)
    for r in range(1, Y):
        total = total + near_in[r].astype(f32)
    for i in range(NF):
        pltpu.make_async_copy(far_in.at[i], far_in.at[i], f2_r.at[i]).wait()
    for i in range(NF):
        total = total + far_in[i].astype(f32)
    kg_ref[...] = (total * (gain_rows * weight))[0:ROWS, :]

    for send in [*gx, *[s for _, s in wx], *c1, *wf, *pairs.values(), *near_sends.values(), *c2]:
        send.wait_send()
    for there, send in [*far_sends, *n2]:
        pl.when(there)(send.wait_send)

    @pl.when(half == c)
    def _():
        for send in f2:
            send.wait_send()

    for out in outs:
        out.wait()


def fused(hidden, w_key, grad_key, gain, counts):
    bf16, f32 = jnp.bfloat16, jnp.float32
    dma = pltpu.SemaphoreType.DMA
    hbm = pl.BlockSpec(memory_space=pltpu.HBM)
    anywhere = pl.BlockSpec(memory_space=pl.ANY)
    return pl.pallas_call(
        kernel,
        out_shape=(
            jax.ShapeDtypeStruct((ROWS, HD), f32),
            jax.ShapeDtypeStruct((TOK, SHARE), bf16),
        ),
        in_specs=[hbm] * 5,
        out_specs=(pl.BlockSpec(memory_space=pltpu.VMEM), anywhere),
        scratch_shapes=[
            pltpu.VMEM((D // 128, 128), f32),
            pltpu.SMEM((1,), jnp.int32),
            pltpu.VMEM((TOK, D), bf16),
            pltpu.VMEM((Z * CHUNK, TOK), bf16),
            pltpu.VMEM((X, SHARE, HD), bf16),
            pltpu.VMEM((X, TOK, HD), bf16),
            pltpu.VMEM((TOK, HD), bf16),
            pltpu.VMEM((TOK, HD), bf16),
            pltpu.VMEM((Z, HALF, TOK), bf16),
            pltpu.VMEM((NF, HALF + 16, HD), f32),
            pltpu.VMEM((Z, HALF, HD), bf16),
            pltpu.VMEM((NF, HALF, HD), bf16),
            pltpu.VMEM((2, HALF, HD), bf16),
            pltpu.VMEM((2, HALF, HD), bf16),
            pltpu.VMEM((4, HALF, HD), bf16),
            pltpu.VMEM((3, NF, FAR, HD), bf16),
            pltpu.VMEM((3, NF, FAR, HD), bf16),
            pltpu.VMEM((4, NF, FAR, HD), bf16),
            pltpu.VMEM((HALF + 8, HD), f32),
            pltpu.VMEM((8, OWN, HD), bf16),
            pltpu.VMEM((NF, FAR + 8, HD), f32),
            pltpu.VMEM((NF, 2, OWN, HD), bf16),
            pltpu.VMEM((Y, OWN, HD), bf16),
            pltpu.VMEM((NF, OWN, HD), bf16),
            pltpu.VMEM((TOK, SHARE), bf16),
            pltpu.VMEM((8, 128), f32),
            pltpu.VMEM((15, 8, 128), f32),
            pltpu.VMEM((8, 128), f32),
            pltpu.VMEM((11, 8, 128), f32),
            dma((8,)), dma((4,)), dma((4,)),
            dma((3,)), dma((3,)), dma((3,)), dma((3,)), dma((3,)), dma((3,)),
            dma((Z + 1,)), dma((Z + 1,)), dma((6,)), dma((6,)), dma((14,)), dma((14,)),
            dma((16,)), dma((8,)), dma((10,)), dma((5,)), dma((15,)), dma((15,)),
            dma((11,)), dma((11,)),
        ],
        compiler_params=pltpu.CompilerParams(
            collective_id=0, has_side_effects=True, vmem_limit_bytes=24 << 20
        ),
    )(hidden, w_key, grad_key, gain, counts)


def per_device(hidden, gain, w_key, grad_key, counts):
    in_hbm = lambda v: pltpu.with_memory_space_constraint(v, pltpu.HBM)
    gain = gain.reshape(D // 128, 128)
    return fused(*(in_hbm(v) for v in (hidden, w_key, grad_key, gain)), counts)


def solution(mesh):
    split = Mesh(
        mesh.devices.reshape(Z, Y, 2, mesh.shape["tensor"]), ("dp_0", "dp_1", "dp_2", "tensor")
    )
    return jax.shard_map(
        per_device,
        mesh=split,
        in_specs=(P(DP, None), P(), P(None, "tensor"), P(DP, "tensor"), P(DP)),
        out_specs=(P(DP, "tensor"), P(DP, "tensor")),
        check_vma=False,
    )
```

```python
import jax
import jax.numpy as jnp
from jax import lax
from jax.experimental import pallas as pl
from jax.experimental.pallas import tpu as pltpu
from jax.sharding import Mesh
from jax.sharding import PartitionSpec as P

DP = ("dp_0", "dp_1", "dp_2")
MESH = pl.DeviceIdType.MESH
EPSILON = 1e-05
Z, Y, X = 12, 8, 4
TOK, D, HD = 128, 8192, 128
ROWS = 43
CHUNK = 16 * ROWS
HALF, LIFT = 352, 336
LEAD = 4
FAR = 96
OWN = 48
FARS = (6, 5, 7, 4, 8)
PARTS = ((0, 2, 1), (2, 5, -1))
GROUPS = (FARS[:2], (3, 9), FARS[2:], (1, 11, 2, 10, 0))
NF = len(FARS)
PIECES = ((0, 12), (12, 24), (24, 36), (36, 48), (48, 56), (56, 60), (60, 64))
SHARE = D // X


def kernel(
    hid_hbm, w_hbm, gk_hbm, gain_hbm, cnt_hbm, kg_ref, ng_hbm,
    gain_ref, cnt_ref, hid, turned, wbuf, heads, scaled, other, pair, shifted, summed, sumfar,
    near_mid, near_out, near, far_mid, far_out, far,
    near_f, near_own, far_f, far_own, near_in, far_in, ngv,
    cnt_own, cnt_in, cnt_mid, cnt_in2,
    hid_sem, loc_sem, out_sem,
    wx_s, wx_r, gx_s, gx_r, wf_s, wf_r, pair_s, pair_r, near_s, near_r, far_s, far_r,
    n2_s, n2_r, f2_s, f2_r, c1_s, c1_r, c2_s, c2_r,
):
    z = lax.axis_index("dp_0")
    y = lax.axis_index("dp_1")
    c = lax.axis_index("dp_2")
    x = lax.axis_index("tensor")
    half, quarter = lax.div(y, 4), lax.rem(y, 4)
    at_z = lambda d: lax.rem(z + d, Z)
    at_y = lambda d: lax.rem(y + d, Y)
    f32, bf16 = jnp.float32, jnp.bfloat16

    def remote(src, dst, ss, rs, zz=None, yy=None, cc=None, xx=None):
        return pltpu.make_async_remote_copy(
            src_ref=src, dst_ref=dst, send_sem=ss, recv_sem=rs,
            device_id=(
                z if zz is None else zz,
                y if yy is None else yy,
                c if cc is None else cc,
                x if xx is None else xx,
            ),
            device_id_type=MESH,
        )

    loads = []
    for i, (first, last) in enumerate(PIECES):
        cols = pl.ds(first * 128, (last - first) * 128)
        load = pltpu.make_async_copy(hid_hbm.at[:, cols], hid.at[:, cols], hid_sem.at[i])
        load.start()
        loads.append(load)
    cnt_load = pltpu.make_async_copy(cnt_hbm, cnt_ref, loc_sem.at[2])
    cnt_load.start()
    gk_load = pltpu.make_async_copy(gk_hbm, heads.at[0], loc_sem.at[0])
    gk_load.start()
    gain_load = pltpu.make_async_copy(gain_hbm, gain_ref, loc_sem.at[3])
    gain_load.start()
    mine = pl.ds(pl.multiple_of(x * SHARE, SHARE), SHARE)
    w_load = pltpu.make_async_copy(w_hbm.at[mine, :], wbuf.at[0], loc_sem.at[1])
    w_load.start()

    barrier = pltpu.get_barrier_semaphore()

    def greet(zz, yy, cc, xx):
        pl.semaphore_signal(barrier, inc=1, device_id=(zz, yy, cc, xx), device_id_type=MESH)

    for d in (6, 5, 7, 4, 8, 3, 9, 2, 10, 1, 11):
        greet(at_z(d), y, c, x)
        if d in FARS:
            greet(at_z(d), y, 1 - c, x)
    for d in (4, 3, 5, 2, 6, 1, 7):
        greet(z, at_y(d), c, x)
        greet(z, at_y(d), 1 - c, x)
    for k in range(1, X):
        greet(z, y, c, lax.rem(x + k, X))
    greet(z, y, 1 - c, x)
    greeted = 1 + 3 + 14 + 11 + NF

    cnt_load.wait()
    count = cnt_ref[0]
    cnt_own[...] = jnp.full((8, 128), count, jnp.int32).astype(f32)
    turned[D:, :] = jnp.zeros((Z * CHUNK - D, TOK), bf16)
    for s in range(NF):
        shifted[s, 0:8, :] = jnp.zeros((8, 128), f32)
        shifted[s, HALF + 8 :, :] = jnp.zeros((8, 128), f32)

    squares = jnp.zeros((TOK, 128), f32)
    for i, (first, last) in enumerate(PIECES):
        loads[i].wait()

        def add_squares(t, total):
            lanes = pl.ds(pl.multiple_of(t * 128, 128), 128)
            block = hid[:, lanes]
            turned[lanes, :] = block.T
            v = block.astype(f32)
            return total + v * v

        squares = lax.fori_loop(first, last, add_squares, squares, unroll=4)
    inv_rms = lax.rsqrt(jnp.sum(squares, axis=1, keepdims=True) * (1.0 / D) + EPSILON)
    live = lax.broadcasted_iota(jnp.int32, (TOK, HD), 0) < count
    gk_load.wait()
    scaled[...] = jnp.where(live, heads[0].astype(f32) * inv_rms, 0.0).astype(bf16)

    pl.semaphore_wait(barrier, greeted)

    near_sends, far_sends = {}, []
    pairs, gx, wx, c1 = {}, [], [], []
    upper = pl.ds(pl.multiple_of(c * (SHARE // 2), SHARE // 2), SHARE // 2)

    def window(target):
        start = lax.div(LEAD + 2 * ROWS * lax.rem(target, 4), 16) * 16
        return pl.ds(pl.multiple_of(start, 16), FAR)

    def here(r):
        return lax.div(at_y(r), 4) == c

    def mine_far(r, first, last):
        return sumfar.at[pl.ds(first, last - first), window(at_y(r)), :]

    def share(j):
        theirs = pl.multiple_of(at_z(j) * CHUNK + (1 - c) * LIFT, 16)
        pairs[j] = remote(
            turned.at[pl.ds(theirs, HALF), :], pair.at[j], pair_s.at[j], pair_r.at[j], cc=1 - c
        )
        pairs[j].start()

    def weights_along_x():
        for k in (1, 3, 2):
            xx = lax.rem(x + k, X)
            theirs = pl.ds(pl.multiple_of(xx * SHARE + c * (SHARE // 2), SHARE // 2), SHARE // 2)
            send = remote(
                w_hbm.at[theirs, :], wbuf.at[k, upper, :], wx_s.at[k - 1], wx_r.at[k - 1], xx=xx
            )
            send.start()
            wx.append((k, send))
        for k in (2, 1, 3):
            xx = lax.rem(x + k, X)
            send = remote(gk_hbm, heads.at[k], gx_s.at[k - 1], gx_r.at[k - 1], xx=xx)
            send.start()
            gx.append(send)

    def counts_along_y():
        for d in range(Y):
            for e in range(2):
                if d + e == 0:
                    continue
                slot = 2 * d + e - 1
                send = remote(
                    cnt_own, cnt_in.at[slot], c1_s.at[slot], c1_r.at[slot],
                    yy=at_y(d), cc=c if e == 0 else 1 - c,
                )
                send.start()
                c1.append(send)

    def send_near(i, src, dst, step):
        near_sends[i] = remote(src, dst, near_s.at[i], near_r.at[i], zz=at_z(step))
        near_sends[i].start()

    def send_far(i, src, dst, r, step):
        send = remote(src, dst, far_s.at[i], far_r.at[i], yy=at_y(step))
        pl.when(here(r))(send.start)
        far_sends.append((here(r), send))

    def finish(group, both):
        tokens = []
        for j in group:
            pairs[j].wait_recv()
            rows = pl.ds(pl.multiple_of(at_z(j) * CHUNK + c * LIFT, 16), HALF)
            tokens.append(jnp.concatenate([turned[rows, :], pair[j]], axis=1))
        total = jnp.dot(jnp.concatenate(tokens, axis=0), both, preferred_element_type=f32)
        for n, j in enumerate(group):
            one = total[n * HALF : (n + 1) * HALF]
            if j in FARS:
                i = FARS.index(j)
                shifted[i, 8 : HALF + 8, :] = one
                sumfar[i] = shifted[i, pl.ds(8 - LEAD + 8 * c, HALF), :].astype(bf16)
            else:
                summed[j] = one.astype(bf16)

    swap = remote(scaled, other, pair_s.at[Z], pair_r.at[Z], cc=1 - c)
    swap.start()
    pairs[Z] = swap
    for group in GROUPS:
        for j in group:
            share(j)
    weights_along_x()
    counts_along_y()
    swap.wait_recv()
    both = jnp.concatenate([scaled[...], other[...]], axis=0)
    def first_far(p):
        first, last, way = PARTS[p]
        n = pl.ds(first, last - first)
        for i, (r, dst, step) in enumerate(
            (
                (4, far_mid.at[0, n], way),
                (-3 * way, far_mid.at[1, n], -way),
                (2 * way, far_mid.at[2, n], way),
                (-way, far.at[0, n], -way),
            )
        ):
            send_far(7 * p + i, mine_far(r % Y, first, last), dst, r % Y, step % Y)

    finish(GROUPS[0], both)
    first_far(0)
    finish(GROUPS[1], both)
    send_near(0, summed.at[3], near_mid.at[0], 1)
    send_near(1, summed.at[9], near_mid.at[1], 11)
    finish(GROUPS[2], both)
    first_far(1)
    finish(GROUPS[3], both)
    send_near(2, summed.at[1], near.at[0], 1)
    send_near(3, summed.at[11], near.at[1], 11)

    def second_far(p):
        first, last, way = PARTS[p]
        n = pl.ds(first, last - first)
        for m, r in enumerate((3 * way % Y, -2 * way % Y, way % Y)):

            @pl.when(here(r))
            def _(p=p, n=n, m=m, r=r, first=first, last=last):
                mid = far_mid.at[m, n]
                pltpu.make_async_copy(mid, mid, far_r.at[7 * p + m]).wait()
                rows = window(at_y(r))
                for i in range(first, last):
                    far_out[m, i] = sumfar[i, rows, :] + far_mid[m, i]

            send_far(7 * p + 4 + m, far_out.at[m, n], far.at[1 + m, n], r, r)

    second_far(0)

    for n, (j, step) in enumerate(((2, 2), (10, 10))):
        near_sends[n].wait_recv()

        def merge_near(t, _, n=n, j=j):
            rows = pl.ds(pl.multiple_of(t * 32, 32), 32)
            near_out[n, rows, :] = summed[j, rows, :] + near_mid[n, rows, :]
            return 0

        lax.fori_loop(0, HALF // 32, merge_near, 0, unroll=True)
        send_near(4 + n, near_out.at[n], near.at[2 + n], step)

    second_far(1)

    for send in c1:
        send.wait_recv()
    cnt_mid[...] = cnt_own[...] + jnp.sum(cnt_in[...], axis=0)
    c2 = []
    for d in range(1, Z):
        send = remote(cnt_mid, cnt_in2.at[d - 1], c2_s.at[d - 1], c2_r.at[d - 1], zz=at_z(d))
        send.start()
        c2.append(send)

    f2 = []
    for i, j in enumerate(FARS):
        for e in range(2):
            f2.append(
                remote(
                    far_own.at[i, e], far_in.at[i], f2_s.at[2 * i + e], f2_r.at[i],
                    zz=at_z(j), cc=e,
                )
            )

    @pl.when(half == c)
    def _():
        rows = window(y)
        start = LEAD + 2 * ROWS * quarter
        inside = start - lax.div(start, 16) * 16
        for p, (first, last, way) in enumerate(PARTS):
            n = pl.ds(first, last - first)
            for slot in range(4):
                come = far.at[slot, n]
                pltpu.make_async_copy(come, come, far_r.at[7 * p + 3 + slot]).wait()
            for i in range(first, last):
                total = sumfar[i, rows, :].astype(f32)
                for slot in range(4):
                    total = total + far[slot, i].astype(f32)
                far_f[i, 0:FAR, :] = total
                for e in range(2):
                    far_own[i, e] = far_f[i, pl.ds(inside + e * ROWS, OWN), :].astype(bf16)
                    f2[2 * i + e].start()

    wf = []

    def pass_on(n):
        k, send = wx[n]
        send.wait_recv()
        forward = remote(
            wbuf.at[k, upper, :], wbuf.at[k, upper, :], wf_s.at[k - 1], wf_r.at[k - 1], cc=1 - c
        )
        forward.start()
        wf.append(forward)

    pass_on(0)
    pass_on(1)

    for i in (2, 3, 4, 5):
        near_sends[i].wait_recv()

    def near_total(t, _):
        rows = pl.ds(pl.multiple_of(t * 32, 32), 32)
        total = summed[0, rows, :].astype(f32)
        for n in range(4):
            total = total + near[n, rows, :].astype(f32)
        near_f[rows, :] = total
        return 0

    lax.fori_loop(0, HALF // 32, near_total, 0, unroll=True)
    for b in range(8):
        near_own[b] = near_f[pl.ds(8 * c + ROWS * b, OWN), :].astype(bf16)
    n2 = []
    for r in (4, 3, 5, 2, 6, 1, 7, 0):
        yy = at_y(r)
        for e in range(2):
            send = remote(
                near_own.at[2 * lax.rem(yy, 4) + e], near_in.at[r], n2_s.at[2 * r + e],
                n2_r.at[r], yy=yy, cc=e,
            )
            there = here(r)
            if r == 0:
                there = jnp.logical_and(there, c != e)
            pl.when(there)(send.start)
            n2.append((there, send))

    @pl.when(half == c)
    def _():
        near_in[0] = near_own[2 * quarter + c]

    pass_on(2)

    gain_load.wait()
    first = ROWS * ((z * Y + y) * 2 + c)
    feature = first + lax.broadcasted_iota(jnp.int32, (OWN, 128), 0)
    lane = lax.broadcasted_iota(jnp.int32, (OWN, 128), 1)
    line = lax.div(first, 128)
    gains = jnp.zeros((OWN, 128), f32)
    for n in range(2):
        at = jnp.minimum(line + n, D // 128 - 1)
        row = gain_ref[pl.ds(at, 1), :]
        gains = jnp.where(feature == at * 128 + lane, row, gains)
    gain_rows = jnp.sum(gains, axis=1, keepdims=True)

    w_load.wait()
    for send in gx:
        send.wait_recv()
    for k in range(X):
        heads[k] = jnp.where(live, heads[k].astype(f32), 0.0).astype(bf16)
    for send in c2:
        send.wait_recv()
    weighting = (1.0 * TOK * Z * Y * 2) / (cnt_mid[...] + jnp.sum(cnt_in2[...], axis=0))
    weight = weighting[0:1, 0:1]
    TILE = 512
    outs = []
    for t in range(SHARE // TILE):
        if 2 * t == SHARE // TILE:
            for forward in wf:
                forward.wait_recv()
        first_half = 2 * t < SHARE // TILE
        base = (c if first_half else 1 - c) * (SHARE // 2) + (t % (SHARE // TILE // 2)) * TILE
        cols = pl.ds(pl.multiple_of(base, TILE), TILE)
        total = None
        for k in range(X):
            term = lax.dot_general(
                heads[k], wbuf[k, cols, :], (((1,), (1,)), ((), ())),
                preferred_element_type=f32,
            )
            total = term if total is None else total + term
        ngv[:, cols] = (total * weight).astype(bf16)
        out = pltpu.make_async_copy(ngv.at[:, cols], ng_hbm.at[:, cols], out_sem.at[t])
        out.start()
        outs.append(out)

    for r in range(1, Y):
        pltpu.make_async_copy(near_in.at[r], near_in.at[r], n2_r.at[r]).wait()

    @pl.when(half != c)
    def _():
        pltpu.make_async_copy(near_in.at[0], near_in.at[0], n2_r.at[0]).wait()

    total = near_in[0].astype(f32)
    for r in range(1, Y):
        total = total + near_in[r].astype(f32)
    for i in range(NF):
        pltpu.make_async_copy(far_in.at[i], far_in.at[i], f2_r.at[i]).wait()
    for i in range(NF):
        total = total + far_in[i].astype(f32)
    kg_ref[...] = (total * (gain_rows * weight))[0:ROWS, :]

    for send in [*gx, *[s for _, s in wx], *c1, *wf, *pairs.values(), *near_sends.values(), *c2]:
        send.wait_send()
    for there, send in [*far_sends, *n2]:
        pl.when(there)(send.wait_send)

    @pl.when(half == c)
    def _():
        for send in f2:
            send.wait_send()

    for out in outs:
        out.wait()


def fused(hidden, w_key, grad_key, gain, counts):
    bf16, f32 = jnp.bfloat16, jnp.float32
    dma = pltpu.SemaphoreType.DMA
    hbm = pl.BlockSpec(memory_space=pltpu.HBM)
    anywhere = pl.BlockSpec(memory_space=pl.ANY)
    return pl.pallas_call(
        kernel,
        out_shape=(
            jax.ShapeDtypeStruct((ROWS, HD), f32),
            jax.ShapeDtypeStruct((TOK, SHARE), bf16),
        ),
        in_specs=[hbm] * 5,
        out_specs=(pl.BlockSpec(memory_space=pltpu.VMEM), anywhere),
        scratch_shapes=[
            pltpu.VMEM((D // 128, 128), f32),
            pltpu.SMEM((1,), jnp.int32),
            pltpu.VMEM((TOK, D), bf16),
            pltpu.VMEM((Z * CHUNK, TOK), bf16),
            pltpu.VMEM((X, SHARE, HD), bf16),
            pltpu.VMEM((X, TOK, HD), bf16),
            pltpu.VMEM((TOK, HD), bf16),
            pltpu.VMEM((TOK, HD), bf16),
            pltpu.VMEM((Z, HALF, TOK), bf16),
            pltpu.VMEM((NF, HALF + 16, HD), f32),
            pltpu.VMEM((Z, HALF, HD), bf16),
            pltpu.VMEM((NF, HALF, HD), bf16),
            pltpu.VMEM((2, HALF, HD), bf16),
            pltpu.VMEM((2, HALF, HD), bf16),
            pltpu.VMEM((4, HALF, HD), bf16),
            pltpu.VMEM((3, NF, FAR, HD), bf16),
            pltpu.VMEM((3, NF, FAR, HD), bf16),
            pltpu.VMEM((4, NF, FAR, HD), bf16),
            pltpu.VMEM((HALF + 8, HD), f32),
            pltpu.VMEM((8, OWN, HD), bf16),
            pltpu.VMEM((NF, FAR + 8, HD), f32),
            pltpu.VMEM((NF, 2, OWN, HD), bf16),
            pltpu.VMEM((Y, OWN, HD), bf16),
            pltpu.VMEM((NF, OWN, HD), bf16),
            pltpu.VMEM((TOK, SHARE), bf16),
            pltpu.VMEM((8, 128), f32),
            pltpu.VMEM((15, 8, 128), f32),
            pltpu.VMEM((8, 128), f32),
            pltpu.VMEM((11, 8, 128), f32),
            dma((8,)), dma((4,)), dma((4,)),
            dma((3,)), dma((3,)), dma((3,)), dma((3,)), dma((3,)), dma((3,)),
            dma((Z + 1,)), dma((Z + 1,)), dma((6,)), dma((6,)), dma((14,)), dma((14,)),
            dma((16,)), dma((8,)), dma((10,)), dma((5,)), dma((15,)), dma((15,)),
            dma((11,)), dma((11,)),
        ],
        compiler_params=pltpu.CompilerParams(
            collective_id=0, has_side_effects=True, vmem_limit_bytes=24 << 20
        ),
    )(hidden, w_key, grad_key, gain, counts)


def put_out(kg, ng):
    def body(kg_ref, ng_ref, kg_hbm, ng_hbm, sems):
        copies = (
            pltpu.make_async_copy(ng_ref, ng_hbm, sems.at[0]),
            pltpu.make_async_copy(kg_ref, kg_hbm, sems.at[1]),
        )
        for copy in copies:
            copy.start()
        for copy in copies:
            copy.wait()

    anywhere = pl.BlockSpec(memory_space=pl.ANY)
    hbm = pl.BlockSpec(memory_space=pltpu.HBM)
    return pl.pallas_call(
        body,
        out_shape=tuple(jax.ShapeDtypeStruct(v.shape, v.dtype) for v in (kg, ng)),
        in_specs=[anywhere] * 2,
        out_specs=(hbm, hbm),
        scratch_shapes=[pltpu.SemaphoreType.DMA((2,))],
        compiler_params=pltpu.CompilerParams(vmem_limit_bytes=1 << 20),
    )(kg, ng)


def per_device(hidden, gain, w_key, grad_key, counts):
    in_hbm = lambda v: pltpu.with_memory_space_constraint(v, pltpu.HBM)
    gain = gain.reshape(D // 128, 128)
    return put_out(*fused(*(in_hbm(v) for v in (hidden, w_key, grad_key, gain)), counts))


def solution(mesh):
    split = Mesh(
        mesh.devices.reshape(Z, Y, 2, mesh.shape["tensor"]), ("dp_0", "dp_1", "dp_2", "tensor")
    )
    return jax.shard_map(
        per_device,
        mesh=split,
        in_specs=(P(DP, None), P(), P(None, "tensor"), P(DP, "tensor"), P(DP)),
        out_specs=(P(DP, "tensor"), P(DP, "tensor")),
        check_vma=False,
    )
```

```python
import jax
import jax.numpy as jnp
from jax import lax
from jax.experimental import pallas as pl
from jax.experimental.pallas import tpu as pltpu
from jax.sharding import Mesh
from jax.sharding import PartitionSpec as P

DP = ("dp_0", "dp_1", "dp_2")
MESH = pl.DeviceIdType.MESH
EPSILON = 1e-05
Z, Y, X = 12, 8, 4
TOK, D, HD = 128, 8192, 128
ROWS = 43
CHUNK = 16 * ROWS
HALF, LIFT = 352, 336
LEAD = 4
FAR = 96
OWN = 48
FARS = (6, 5, 7, 4, 8)
PARTS = ((0, 2, 1), (2, 5, -1))
GROUPS = (FARS[:2], (3, 9), FARS[2:], (1, 11, 2, 10, 0))
NF = len(FARS)
PIECES = ((0, 12), (12, 24), (24, 36), (36, 48), (48, 56), (56, 60), (60, 64))
SHARE = D // X


def kernel(
    hid_hbm, w_hbm, gk_hbm, gain_hbm, cnt_hbm, kg_ref, ng_hbm,
    gain_ref, cnt_ref, hid, turned, wbuf, heads, scaled, other, pair, shifted, summed, sumfar,
    near_mid, near_out, near, far_mid, far_out, far,
    near_f, near_own, far_f, far_own, near_in, far_in, ngv,
    cnt_own, cnt_in, cnt_mid, cnt_in2,
    hid_sem, loc_sem, out_sem,
    wx_s, wx_r, gx_s, gx_r, wf_s, wf_r, pair_s, pair_r, near_s, near_r, far_s, far_r,
    n2_s, n2_r, f2_s, f2_r, c1_s, c1_r, c2_s, c2_r,
):
    z = lax.axis_index("dp_0")
    y = lax.axis_index("dp_1")
    c = lax.axis_index("dp_2")
    x = lax.axis_index("tensor")
    half, quarter = lax.div(y, 4), lax.rem(y, 4)
    at_z = lambda d: lax.rem(z + d, Z)
    at_y = lambda d: lax.rem(y + d, Y)
    f32, bf16 = jnp.float32, jnp.bfloat16

    def remote(src, dst, ss, rs, zz=None, yy=None, cc=None, xx=None):
        return pltpu.make_async_remote_copy(
            src_ref=src, dst_ref=dst, send_sem=ss, recv_sem=rs,
            device_id=(
                z if zz is None else zz,
                y if yy is None else yy,
                c if cc is None else cc,
                x if xx is None else xx,
            ),
            device_id_type=MESH,
        )

    loads = []
    for i, (first, last) in enumerate(PIECES):
        cols = pl.ds(first * 128, (last - first) * 128)
        load = pltpu.make_async_copy(hid_hbm.at[:, cols], hid.at[:, cols], hid_sem.at[i])
        load.start()
        loads.append(load)
    cnt_load = pltpu.make_async_copy(cnt_hbm, cnt_ref, loc_sem.at[2])
    cnt_load.start()
    gk_load = pltpu.make_async_copy(gk_hbm, heads.at[0], loc_sem.at[0])
    gk_load.start()
    gain_load = pltpu.make_async_copy(gain_hbm, gain_ref, loc_sem.at[3])
    gain_load.start()
    mine = pl.ds(pl.multiple_of(x * SHARE, SHARE), SHARE)
    w_load = pltpu.make_async_copy(w_hbm.at[mine, :], wbuf.at[0], loc_sem.at[1])
    w_load.start()

    barrier = pltpu.get_barrier_semaphore()

    def greet(zz, yy, cc, xx):
        pl.semaphore_signal(barrier, inc=1, device_id=(zz, yy, cc, xx), device_id_type=MESH)

    for d in (6, 5, 7, 4, 8, 3, 9, 2, 10, 1, 11):
        greet(at_z(d), y, c, x)
        if d in FARS:
            greet(at_z(d), y, 1 - c, x)
    for d in (4, 3, 5, 2, 6, 1, 7):
        greet(z, at_y(d), c, x)
        greet(z, at_y(d), 1 - c, x)
    for k in range(1, X):
        greet(z, y, c, lax.rem(x + k, X))
    greet(z, y, 1 - c, x)
    greeted = 1 + 3 + 14 + 11 + NF

    cnt_load.wait()
    count = cnt_ref[0]
    cnt_own[...] = jnp.full((8, 128), count, jnp.int32).astype(f32)
    turned[D:, :] = jnp.zeros((Z * CHUNK - D, TOK), bf16)
    for s in range(NF):
        shifted[s, 0:8, :] = jnp.zeros((8, 128), f32)
        shifted[s, HALF + 8 :, :] = jnp.zeros((8, 128), f32)

    squares = jnp.zeros((TOK, 128), f32)
    for i, (first, last) in enumerate(PIECES):
        loads[i].wait()

        def add_squares(t, total):
            lanes = pl.ds(pl.multiple_of(t * 128, 128), 128)
            block = hid[:, lanes]
            turned[lanes, :] = block.T
            v = block.astype(f32)
            return total + v * v

        squares = lax.fori_loop(first, last, add_squares, squares, unroll=4)
    inv_rms = lax.rsqrt(jnp.sum(squares, axis=1, keepdims=True) * (1.0 / D) + EPSILON)
    live = lax.broadcasted_iota(jnp.int32, (TOK, HD), 0) < count
    gk_load.wait()
    scaled[...] = jnp.where(live, heads[0].astype(f32) * inv_rms, 0.0).astype(bf16)

    pl.semaphore_wait(barrier, greeted)

    near_sends, far_sends = {}, []
    pairs, gx, wx, c2 = {}, [], [], []
    upper = pl.ds(pl.multiple_of(c * (SHARE // 2), SHARE // 2), SHARE // 2)

    def window(target):
        start = lax.div(LEAD + 2 * ROWS * lax.rem(target, 4), 16) * 16
        return pl.ds(pl.multiple_of(start, 16), FAR)

    def here(r):
        return lax.div(at_y(r), 4) == c

    def mine_far(r, first, last):
        return sumfar.at[pl.ds(first, last - first), window(at_y(r)), :]

    def share(j):
        theirs = pl.multiple_of(at_z(j) * CHUNK + (1 - c) * LIFT, 16)
        pairs[j] = remote(
            turned.at[pl.ds(theirs, HALF), :], pair.at[j], pair_s.at[j], pair_r.at[j], cc=1 - c
        )
        pairs[j].start()

    def weights_along_x():
        for k in (1, 3, 2):
            xx = lax.rem(x + k, X)
            theirs = pl.ds(pl.multiple_of(xx * SHARE + c * (SHARE // 2), SHARE // 2), SHARE // 2)
            send = remote(
                w_hbm.at[theirs, :], wbuf.at[k, upper, :], wx_s.at[k - 1], wx_r.at[k - 1], xx=xx
            )
            send.start()
            wx.append((k, send))
        for k in (2, 1, 3):
            xx = lax.rem(x + k, X)
            send = remote(gk_hbm, heads.at[k], gx_s.at[k - 1], gx_r.at[k - 1], xx=xx)
            send.start()
            gx.append(send)

    def counts_along_z():
        for d in range(1, Z):
            send = remote(cnt_own, cnt_in2.at[d - 1], c2_s.at[d - 1], c2_r.at[d - 1], zz=at_z(d))
            send.start()
            c2.append(send)

    def send_near(i, src, dst, step):
        near_sends[i] = remote(src, dst, near_s.at[i], near_r.at[i], zz=at_z(step))
        near_sends[i].start()

    def send_far(i, src, dst, r, step):
        send = remote(src, dst, far_s.at[i], far_r.at[i], yy=at_y(step))
        pl.when(here(r))(send.start)
        far_sends.append((here(r), send))

    def finish(group, both):
        tokens = []
        for j in group:
            pairs[j].wait_recv()
            rows = pl.ds(pl.multiple_of(at_z(j) * CHUNK + c * LIFT, 16), HALF)
            tokens.append(jnp.concatenate([turned[rows, :], pair[j]], axis=1))
        total = jnp.dot(jnp.concatenate(tokens, axis=0), both, preferred_element_type=f32)
        for n, j in enumerate(group):
            one = total[n * HALF : (n + 1) * HALF]
            if j in FARS:
                i = FARS.index(j)
                shifted[i, 8 : HALF + 8, :] = one
                sumfar[i] = shifted[i, pl.ds(8 - LEAD + 8 * c, HALF), :].astype(bf16)
            else:
                summed[j] = one.astype(bf16)

    swap = remote(scaled, other, pair_s.at[Z], pair_r.at[Z], cc=1 - c)
    swap.start()
    pairs[Z] = swap
    for group in GROUPS:
        for j in group:
            share(j)
    weights_along_x()
    counts_along_z()
    swap.wait_recv()
    both = jnp.concatenate([scaled[...], other[...]], axis=0)
    def first_far(p):
        first, last, way = PARTS[p]
        n = pl.ds(first, last - first)
        for i, (r, dst, step) in enumerate(
            (
                (4, far_mid.at[0, n], way),
                (-3 * way, far_mid.at[1, n], -way),
                (2 * way, far_mid.at[2, n], way),
                (-way, far.at[0, n], -way),
            )
        ):
            send_far(7 * p + i, mine_far(r % Y, first, last), dst, r % Y, step % Y)

    finish(GROUPS[0], both)
    first_far(0)
    finish(GROUPS[1], both)
    send_near(0, summed.at[3], near_mid.at[0], 1)
    send_near(1, summed.at[9], near_mid.at[1], 11)
    finish(GROUPS[2], both)
    first_far(1)
    finish(GROUPS[3], both)
    send_near(2, summed.at[1], near.at[0], 1)
    send_near(3, summed.at[11], near.at[1], 11)

    def second_far(p):
        first, last, way = PARTS[p]
        n = pl.ds(first, last - first)
        for m, r in enumerate((3 * way % Y, -2 * way % Y, way % Y)):

            @pl.when(here(r))
            def _(p=p, n=n, m=m, r=r, first=first, last=last):
                mid = far_mid.at[m, n]
                pltpu.make_async_copy(mid, mid, far_r.at[7 * p + m]).wait()
                rows = window(at_y(r))
                for i in range(first, last):
                    far_out[m, i] = sumfar[i, rows, :] + far_mid[m, i]

            send_far(7 * p + 4 + m, far_out.at[m, n], far.at[1 + m, n], r, r)

    second_far(0)

    for n, (j, step) in enumerate(((2, 2), (10, 10))):
        near_sends[n].wait_recv()

        def merge_near(t, _, n=n, j=j):
            rows = pl.ds(pl.multiple_of(t * 32, 32), 32)
            near_out[n, rows, :] = summed[j, rows, :] + near_mid[n, rows, :]
            return 0

        lax.fori_loop(0, HALF // 32, merge_near, 0, unroll=True)
        send_near(4 + n, near_out.at[n], near.at[2 + n], step)

    second_far(1)

    for send in c2:
        send.wait_recv()
    cnt_mid[...] = cnt_own[...] + jnp.sum(cnt_in2[...], axis=0)
    c1 = []
    for d in range(Y):
        for e in range(2):
            if d + e == 0:
                continue
            slot = 2 * d + e - 1
            send = remote(
                cnt_mid, cnt_in.at[slot], c1_s.at[slot], c1_r.at[slot],
                yy=at_y(d), cc=c if e == 0 else 1 - c,
            )
            send.start()
            c1.append(send)

    f2 = []
    for i, j in enumerate(FARS):
        for e in range(2):
            f2.append(
                remote(
                    far_own.at[i, e], far_in.at[i], f2_s.at[2 * i + e], f2_r.at[i],
                    zz=at_z(j), cc=e,
                )
            )

    @pl.when(half == c)
    def _():
        rows = window(y)
        start = LEAD + 2 * ROWS * quarter
        inside = start - lax.div(start, 16) * 16
        for p, (first, last, way) in enumerate(PARTS):
            n = pl.ds(first, last - first)
            for slot in range(4):
                come = far.at[slot, n]
                pltpu.make_async_copy(come, come, far_r.at[7 * p + 3 + slot]).wait()
            for i in range(first, last):
                total = sumfar[i, rows, :].astype(f32)
                for slot in range(4):
                    total = total + far[slot, i].astype(f32)
                far_f[i, 0:FAR, :] = total
                for e in range(2):
                    far_own[i, e] = far_f[i, pl.ds(inside + e * ROWS, OWN), :].astype(bf16)
                    f2[2 * i + e].start()

    wf = []

    def pass_on(n):
        k, send = wx[n]
        send.wait_recv()
        forward = remote(
            wbuf.at[k, upper, :], wbuf.at[k, upper, :], wf_s.at[k - 1], wf_r.at[k - 1], cc=1 - c
        )
        forward.start()
        wf.append(forward)

    pass_on(0)
    pass_on(1)

    for i in (2, 3, 4, 5):
        near_sends[i].wait_recv()

    def near_total(t, _):
        rows = pl.ds(pl.multiple_of(t * 32, 32), 32)
        total = summed[0, rows, :].astype(f32)
        for n in range(4):
            total = total + near[n, rows, :].astype(f32)
        near_f[rows, :] = total
        return 0

    lax.fori_loop(0, HALF // 32, near_total, 0, unroll=True)
    for b in range(8):
        near_own[b] = near_f[pl.ds(8 * c + ROWS * b, OWN), :].astype(bf16)
    n2 = []
    for r in (4, 3, 5, 2, 6, 1, 7, 0):
        yy = at_y(r)
        for e in range(2):
            send = remote(
                near_own.at[2 * lax.rem(yy, 4) + e], near_in.at[r], n2_s.at[2 * r + e],
                n2_r.at[r], yy=yy, cc=e,
            )
            there = here(r)
            if r == 0:
                there = jnp.logical_and(there, c != e)
            pl.when(there)(send.start)
            n2.append((there, send))

    @pl.when(half == c)
    def _():
        near_in[0] = near_own[2 * quarter + c]

    pass_on(2)

    gain_load.wait()
    first = ROWS * ((z * Y + y) * 2 + c)
    feature = first + lax.broadcasted_iota(jnp.int32, (OWN, 128), 0)
    lane = lax.broadcasted_iota(jnp.int32, (OWN, 128), 1)
    line = lax.div(first, 128)
    gains = jnp.zeros((OWN, 128), f32)
    for n in range(2):
        at = jnp.minimum(line + n, D // 128 - 1)
        row = gain_ref[pl.ds(at, 1), :]
        gains = jnp.where(feature == at * 128 + lane, row, gains)
    gain_rows = jnp.sum(gains, axis=1, keepdims=True)

    w_load.wait()
    for send in gx:
        send.wait_recv()
    for k in range(X):
        heads[k] = jnp.where(live, heads[k].astype(f32), 0.0).astype(bf16)
    for send in c1:
        send.wait_recv()
    weighting = (1.0 * TOK * Z * Y * 2) / (cnt_mid[...] + jnp.sum(cnt_in[...], axis=0))
    weight = weighting[0:1, 0:1]
    TILE = 512
    outs = []
    for t in range(SHARE // TILE):
        if 2 * t == SHARE // TILE:
            for forward in wf:
                forward.wait_recv()
        first_half = 2 * t < SHARE // TILE
        base = (c if first_half else 1 - c) * (SHARE // 2) + (t % (SHARE // TILE // 2)) * TILE
        cols = pl.ds(pl.multiple_of(base, TILE), TILE)
        total = None
        for k in range(X):
            term = lax.dot_general(
                heads[k], wbuf[k, cols, :], (((1,), (1,)), ((), ())),
                preferred_element_type=f32,
            )
            total = term if total is None else total + term
        ngv[:, cols] = (total * weight).astype(bf16)
        out = pltpu.make_async_copy(ngv.at[:, cols], ng_hbm.at[:, cols], out_sem.at[t])
        out.start()
        outs.append(out)

    for r in range(1, Y):
        pltpu.make_async_copy(near_in.at[r], near_in.at[r], n2_r.at[r]).wait()

    @pl.when(half != c)
    def _():
        pltpu.make_async_copy(near_in.at[0], near_in.at[0], n2_r.at[0]).wait()

    total = near_in[0].astype(f32)
    for r in range(1, Y):
        total = total + near_in[r].astype(f32)
    for i in range(NF):
        pltpu.make_async_copy(far_in.at[i], far_in.at[i], f2_r.at[i]).wait()
    for i in range(NF):
        total = total + far_in[i].astype(f32)
    kg_ref[...] = (total * (gain_rows * weight))[0:ROWS, :]

    for send in [*gx, *[s for _, s in wx], *c1, *wf, *pairs.values(), *near_sends.values(), *c2]:
        send.wait_send()
    for there, send in [*far_sends, *n2]:
        pl.when(there)(send.wait_send)

    @pl.when(half == c)
    def _():
        for send in f2:
            send.wait_send()

    for out in outs:
        out.wait()


def fused(hidden, w_key, grad_key, gain, counts):
    bf16, f32 = jnp.bfloat16, jnp.float32
    dma = pltpu.SemaphoreType.DMA
    hbm = pl.BlockSpec(memory_space=pltpu.HBM)
    anywhere = pl.BlockSpec(memory_space=pl.ANY)
    return pl.pallas_call(
        kernel,
        out_shape=(
            jax.ShapeDtypeStruct((ROWS, HD), f32),
            jax.ShapeDtypeStruct((TOK, SHARE), bf16),
        ),
        in_specs=[hbm] * 5,
        out_specs=(pl.BlockSpec(memory_space=pltpu.VMEM), anywhere),
        scratch_shapes=[
            pltpu.VMEM((D // 128, 128), f32),
            pltpu.SMEM((1,), jnp.int32),
            pltpu.VMEM((TOK, D), bf16),
            pltpu.VMEM((Z * CHUNK, TOK), bf16),
            pltpu.VMEM((X, SHARE, HD), bf16),
            pltpu.VMEM((X, TOK, HD), bf16),
            pltpu.VMEM((TOK, HD), bf16),
            pltpu.VMEM((TOK, HD), bf16),
            pltpu.VMEM((Z, HALF, TOK), bf16),
            pltpu.VMEM((NF, HALF + 16, HD), f32),
            pltpu.VMEM((Z, HALF, HD), bf16),
            pltpu.VMEM((NF, HALF, HD), bf16),
            pltpu.VMEM((2, HALF, HD), bf16),
            pltpu.VMEM((2, HALF, HD), bf16),
            pltpu.VMEM((4, HALF, HD), bf16),
            pltpu.VMEM((3, NF, FAR, HD), bf16),
            pltpu.VMEM((3, NF, FAR, HD), bf16),
            pltpu.VMEM((4, NF, FAR, HD), bf16),
            pltpu.VMEM((HALF + 8, HD), f32),
            pltpu.VMEM((8, OWN, HD), bf16),
            pltpu.VMEM((NF, FAR + 8, HD), f32),
            pltpu.VMEM((NF, 2, OWN, HD), bf16),
            pltpu.VMEM((Y, OWN, HD), bf16),
            pltpu.VMEM((NF, OWN, HD), bf16),
            pltpu.VMEM((TOK, SHARE), bf16),
            pltpu.VMEM((8, 128), f32),
            pltpu.VMEM((15, 8, 128), f32),
            pltpu.VMEM((8, 128), f32),
            pltpu.VMEM((11, 8, 128), f32),
            dma((8,)), dma((4,)), dma((4,)),
            dma((3,)), dma((3,)), dma((3,)), dma((3,)), dma((3,)), dma((3,)),
            dma((Z + 1,)), dma((Z + 1,)), dma((6,)), dma((6,)), dma((14,)), dma((14,)),
            dma((16,)), dma((8,)), dma((10,)), dma((5,)), dma((15,)), dma((15,)),
            dma((11,)), dma((11,)),
        ],
        compiler_params=pltpu.CompilerParams(
            collective_id=0, has_side_effects=True, vmem_limit_bytes=24 << 20
        ),
    )(hidden, w_key, grad_key, gain, counts)


def put_out(kg, ng):
    def body(kg_ref, ng_ref, kg_hbm, ng_hbm, sems):
        copies = (
            pltpu.make_async_copy(ng_ref, ng_hbm, sems.at[0]),
            pltpu.make_async_copy(kg_ref, kg_hbm, sems.at[1]),
        )
        for copy in copies:
            copy.start()
        for copy in copies:
            copy.wait()

    anywhere = pl.BlockSpec(memory_space=pl.ANY)
    hbm = pl.BlockSpec(memory_space=pltpu.HBM)
    return pl.pallas_call(
        body,
        out_shape=tuple(jax.ShapeDtypeStruct(v.shape, v.dtype) for v in (kg, ng)),
        in_specs=[anywhere] * 2,
        out_specs=(hbm, hbm),
        scratch_shapes=[pltpu.SemaphoreType.DMA((2,))],
        compiler_params=pltpu.CompilerParams(vmem_limit_bytes=1 << 20),
    )(kg, ng)


def per_device(hidden, gain, w_key, grad_key, counts):
    in_hbm = lambda v: pltpu.with_memory_space_constraint(v, pltpu.HBM)
    gain = gain.reshape(D // 128, 128)
    return put_out(*fused(*(in_hbm(v) for v in (hidden, w_key, grad_key, gain)), counts))


def solution(mesh):
    split = Mesh(
        mesh.devices.reshape(Z, Y, 2, mesh.shape["tensor"]), ("dp_0", "dp_1", "dp_2", "tensor")
    )
    return jax.shard_map(
        per_device,
        mesh=split,
        in_specs=(P(DP, None), P(), P(None, "tensor"), P(DP, "tensor"), P(DP)),
        out_specs=(P(DP, "tensor"), P(DP, "tensor")),
        check_vma=False,
    )
```
